256 devices in a mesh: samp: 8 (over y, core), par: 32 (over z, x).
Axes of the slice: x: 4, y: 4, z: 8, core: 2. Of those that a mesh axis runs over, the one named last changes fastest.
Arguments:
- jacobian: bfloat16 [8192, 65536], P(('samp', 'par')), as said below
- sample_slot: int32 [8192], P(('samp', 'par')), may hold values from 0 to 1023, as said below
- panel_index: int32 [1], replicated, may hold values from 0 to 8191
- shift_value: float32 [1], replicated, may hold values from 0.1 to 1
Outputs:
- cholesky_panel: float32 [8192, 1024], P(('samp', 'par'))
The draws below stay inside these ranges and needn't reach their ends.
Inputs may be any that keep to these rules, and one draw needn't show every extreme that they name: Within each group (samples g * 1024 to (g + 1) * 1024 - 1), sample_slot is a permutation of 0 to 1023. `jacobian`: finite values.
All inputs are finite; a program needn't handle non-finite values.
Results may differ from the reference program's by a relative error of at most 0.0003.
Values may be sent and summed in bfloat16 or wider, within the bound.
A program may use at most 128 MiB of HBM per device.

```python
import math
import jax
import jax.numpy as jnp
from jax import lax

PARAMS = 65536
GROUP = 1024
GROUPS = 8
SAMPLES = 8192


def draw_jacobian(key, part):
    shared_count = 16
    first, second, third = jax.random.split(jax.random.fold_in(key, 11), 3)
    noise = jax.random.normal(first, (SAMPLES, PARAMS), jnp.float32)
    coefs = jax.random.normal(second, (SAMPLES, shared_count), jnp.float32)
    directions = jax.random.normal(third, (shared_count, PARAMS), jnp.float32)
    common = jnp.dot(coefs, directions) / jnp.sqrt(jnp.float32(shared_count))
    total = (noise + common) * jnp.sqrt(jnp.float32(SAMPLES) / jnp.float32(PARAMS))
    return total.astype(jnp.bfloat16)


def draw_sample_slot(key, part):
    base = jax.random.fold_in(key, 23)

    def one_group(index):
        return jax.random.permutation(jax.random.fold_in(base, index), GROUP).astype(jnp.int32)
    return jax.vmap(one_group)(jnp.arange(GROUPS, dtype=jnp.int32)).reshape(SAMPLES)


def setup_inputs(seed: int = 0) -> dict:
    keys = jax.random.split(jax.random.key(seed), 5)
    jacobian = draw_jacobian(jax.random.fold_in(keys[4], 71), 0)
    sample_slot = draw_sample_slot(jax.random.fold_in(keys[4], 71), 0)
    panel_index = jax.random.randint(keys[2], (1,), 0, SAMPLES).astype(jnp.int32)
    shift_value = jnp.clip(jnp.exp(jax.random.uniform(keys[3], (1,), jnp.float32, math.log(0.1), math.log(1.0))), 0.1, 1.0)
    return {"jacobian": jacobian, "sample_slot": sample_slot, "panel_index": panel_index, "shift_value": shift_value}


def reference(jacobian, sample_slot, panel_index, shift_value):
    grouped = jacobian.reshape(GROUPS, GROUP, PARAMS)
    slots = sample_slot.reshape(GROUPS, GROUP)
    inverse = jnp.argsort(slots, axis=1).astype(jnp.int32)
    ordered = jnp.take_along_axis(grouped, inverse[:, :, None], axis=1)
    pivot_group = panel_index[0] // GROUP
    rotation = panel_index[0] % GROUP
    pivot = jnp.roll(lax.dynamic_index_in_dim(ordered, pivot_group, 0, keepdims=False), -rotation, axis=0)
    identity_matrix = jnp.eye(GROUP, dtype=jnp.float32)
    shifted_eye = jnp.roll(identity_matrix, -rotation, axis=1)
    group_ids = jnp.arange(GROUPS, dtype=jnp.int32)

    def one_block(pair):
        rows, gid = pair
        product = lax.dot_general(rows.astype(jnp.float32), pivot.astype(jnp.float32), (((1,), (1,)), ((), ())), preferred_element_type=jnp.float32)
        on_pivot = (gid == pivot_group).astype(jnp.float32)
        return product / SAMPLES + shift_value[0] * on_pivot * shifted_eye
    gram = lax.map(one_block, (ordered, group_ids))
    block = jnp.roll(lax.dynamic_index_in_dim(gram, pivot_group, 0, keepdims=False), -rotation, axis=0)
    factor = jnp.linalg.cholesky(block)
    inverse_factor = lax.linalg.triangular_solve(factor, identity_matrix, left_side=True, lower=True)
    flat = gram.reshape(SAMPLES, GROUP)
    return lax.dot_general(flat.astype(jnp.float32), inverse_factor.astype(jnp.float32), (((1,), (1,)), ((), ())), precision=lax.Precision.HIGHEST, preferred_element_type=jnp.float32)
```

```python
import jax
import jax.numpy as jnp
from jax import lax
from jax.experimental import pallas as pl
from jax.experimental.pallas import tpu as pltpu
from jax.sharding import Mesh
from jax.sharding import PartitionSpec as P

PAR = ("z", "x")
PLANE = ("samp", "x")
ALL = ("samp", "z", "x")
NB = 128
HI = lax.Precision.HIGHEST


def rank_update(r):
    h = r.astype(jnp.bfloat16).astype(jnp.float32)
    m = (r - h).astype(jnp.bfloat16).astype(jnp.float32)
    l = (r - h - m).astype(jnp.bfloat16).astype(jnp.float32)
    lhs = jnp.concatenate([h, h, m, h, l, m], 0).astype(jnp.bfloat16)
    rhs = jnp.concatenate([h, m, h, l, h, m], 0).astype(jnp.bfloat16)
    return lax.dot_general(
        lhs, rhs, (((0,), (0,)), ((), ())), preferred_element_type=jnp.float32
    )


def inverse_of_factor(block):
    n = block.shape[0]
    groups = n // 8
    rows = [block[8 * i : 8 * i + 8, :] for i in range(groups)]
    sub = lax.broadcasted_iota(jnp.int32, (8, n), 0)
    lane = lax.broadcasted_iota(jnp.int32, (8, n), 1)
    for b in range(groups):
        r = rows[b]
        cols = [jnp.broadcast_to(r[:, 8 * b + j : 8 * b + j + 1], (8, n)) for j in range(8)]
        inside = (lane >= 8 * b) & (lane < 8 * b + 8)
        r = jnp.where(inside, jnp.where(lane == sub + 8 * b, 1.0, 0.0), r)
        diag = jnp.ones((8, n), jnp.float32)
        for j in range(8):
            d = jnp.broadcast_to(cols[j][j : j + 1, :], (8, n))
            diag = jnp.where(sub == j, d, diag)
            if j < 7:
                q = pl.reciprocal(d, approx=True)
                q = q * (2.0 - d * q)
                m = jnp.where(sub > j, cols[j] * q, 0.0)
                for c in range(j + 1, 8):
                    cols[c] = cols[c] - m * jnp.broadcast_to(cols[c][j : j + 1, :], (8, n))
                r = r - m * jnp.broadcast_to(r[j : j + 1, :], (8, n))
        s = lax.rsqrt(diag)
        s = s * (1.5 - 0.5 * diag * s * s)
        r = r * s
        rows[b] = r
        if b < groups - 1:
            p = rank_update(r)
            for i in range(b + 1, groups):
                rows[i] = jnp.where(inside, 0.0, rows[i]) - p[8 * i : 8 * i + 8, :]
    kept = [jnp.where(lane <= sub + 8 * b, rows[b], 0.0) for b in range(groups)]
    return jnp.concatenate(kept, 0)


def times_transposed(a, b):
    return lax.dot_general(
        a, b, (((1,), (1,)), ((), ())), precision=HI, preferred_element_type=jnp.float32
    )


def factor_kernel(a_ref, o_ref):
    n = a_ref.shape[0]
    steps = n // NB
    o_ref[...] = a_ref[...]
    for kb in range(steps):
        own = slice(kb * NB, kb * NB + NB)
        w = inverse_of_factor(o_ref[own, own])
        o_ref[own, own] = w
        if kb == steps - 1:
            break
        lo = (kb + 1) * NB
        o_ref[lo:, own] = times_transposed(o_ref[lo:, own], w)
        for j in range(kb + 1, steps):
            cj = slice(j * NB, j * NB + NB)
            o_ref[j * NB :, cj] = o_ref[j * NB :, cj] - times_transposed(
                o_ref[j * NB :, own], o_ref[cj, own]
            )


def factored(block):
    vmem = pl.BlockSpec(memory_space=pltpu.VMEM)
    n = block.shape[0]
    return pl.pallas_call(
        factor_kernel,
        out_shape=jax.ShapeDtypeStruct(block.shape, jnp.float32),
        in_specs=[vmem],
        out_specs=vmem,
        cost_estimate=pl.CostEstimate(flops=40 * n**3, bytes_accessed=8 * n * n, transcendentals=0),
        name="factor",
    )(block)


def solve_kernel(g_ref, f_ref, o_ref):
    n = f_ref.shape[0]
    o_ref[...] = g_ref[...]
    for kb in range(n // NB):
        own = slice(kb * NB, kb * NB + NB)
        x = times_transposed(o_ref[:, own], f_ref[own, own])
        o_ref[:, own] = x
        lo = (kb + 1) * NB
        if lo < n:
            o_ref[:, lo:] = o_ref[:, lo:] - times_transposed(x, f_ref[lo:, own])


def solved(rows, factor):
    vmem = pl.BlockSpec(memory_space=pltpu.VMEM)
    return pl.pallas_call(
        solve_kernel,
        out_shape=jax.ShapeDtypeStruct(rows.shape, jnp.float32),
        in_specs=[vmem, vmem],
        out_specs=vmem,
        name="solve",
    )(rows, factor)


def on_device(jacobian, sample_slot, panel_index, shift_value):
    width = sample_slot.shape[0]
    group_width = width * lax.axis_size(PAR)
    samples = group_width * lax.axis_size("samp")
    pivot_group = panel_index[0] // group_width
    rotation = panel_index[0] % group_width
    slots = lax.all_gather(sample_slot, ALL, axis=0, tiled=True)
    slots = slots.reshape(-1, group_width)
    own_slots = lax.dynamic_index_in_dim(slots, lax.axis_index("samp"), 0, keepdims=False)
    pivot_slots = lax.dynamic_index_in_dim(slots, pivot_group, 0, keepdims=False)
    column = jnp.arange(group_width, dtype=jnp.int32)
    chosen = (pivot_slots[None, :] == ((column + rotation) % group_width)[:, None]).astype(jnp.bfloat16)

    tile = lax.all_to_all(jacobian, PLANE, split_axis=1, concat_axis=0, tiled=True)
    band = group_width // lax.axis_size("z")
    mine = lax.dynamic_slice_in_dim(tile, pivot_group * band, band, 0)
    raw = lax.all_gather(mine, "z", axis=0, tiled=True)
    pivot = lax.dot_general(
        chosen, raw, (((1,), (0,)), ((), ())), preferred_element_type=jnp.float32
    ).astype(jnp.bfloat16)

    contract = (((1,), (1,)), ((), ()))
    part = lax.dynamic_slice_in_dim(pivot, lax.axis_index("z") * band, band, 0)
    pivot_part = lax.dot_general(part, pivot, contract, preferred_element_type=jnp.float32)
    pivot_share = lax.psum_scatter(pivot_part, PLANE, scatter_dimension=0, tiled=True)
    block = lax.all_gather(pivot_share, ("z", "samp", "x"), axis=0, tiled=True)
    identity_matrix = jnp.eye(group_width, dtype=jnp.float32)
    block = block / samples + shift_value[0] * identity_matrix

    partial = lax.dot_general(tile, pivot, contract, preferred_element_type=jnp.float32)
    rows = lax.psum_scatter(partial, PLANE, scatter_dimension=0, tiled=True)
    group_rows = lax.all_gather(rows, PAR, axis=0, tiled=True)
    position = lax.axis_index(PAR) * width + jnp.arange(width, dtype=jnp.int32)
    hit = own_slots[None, :] == position[:, None]
    source = jnp.sum(jnp.where(hit, column[None, :], 0), axis=1)
    my_rows = jnp.take(group_rows, source, axis=0) / samples
    on_pivot = lax.axis_index("samp") == pivot_group
    shifted = position[:, None] == ((column + rotation) % group_width)[None, :]
    my_rows = my_rows + jnp.where(shifted & on_pivot, shift_value[0], 0.0)
    return solved(my_rows, factored(block))


def solution(mesh):
    torus = Mesh(mesh.devices.reshape(mesh.shape["samp"], 8, 4), ("samp", "z", "x"))
    return jax.shard_map(
        on_device,
        mesh=torus,
        in_specs=(P(ALL, None), P(ALL), P(), P()),
        out_specs=P(ALL, None),
        check_vma=False,
    )
```

```python
import jax
import jax.numpy as jnp
from jax import lax
from jax.experimental import pallas as pl
from jax.experimental.pallas import tpu as pltpu
from jax.sharding import Mesh
from jax.sharding import PartitionSpec as P

PAR = ("z", "x")
PLANE = ("samp", "x")
ALL = ("samp", "z", "x")
NB = 128
HI = lax.Precision.HIGHEST


def rank_update(r):
    h = r.astype(jnp.bfloat16).astype(jnp.float32)
    m = (r - h).astype(jnp.bfloat16).astype(jnp.float32)
    l = (r - h - m).astype(jnp.bfloat16).astype(jnp.float32)
    lhs = jnp.concatenate([h, h, m, h, l, m], 0).astype(jnp.bfloat16)
    rhs = jnp.concatenate([h, m, h, l, h, m], 0).astype(jnp.bfloat16)
    return lax.dot_general(
        lhs, rhs, (((0,), (0,)), ((), ())), preferred_element_type=jnp.float32
    )


def inverse_of_factor(block):
    n = block.shape[0]
    groups = n // 8
    rows = [block[8 * i : 8 * i + 8, :] for i in range(groups)]
    sub = lax.broadcasted_iota(jnp.int32, (8, n), 0)
    lane = lax.broadcasted_iota(jnp.int32, (8, n), 1)
    for b in range(groups):
        r = rows[b]
        cols = [jnp.broadcast_to(r[:, 8 * b + j : 8 * b + j + 1], (8, n)) for j in range(8)]
        inside = (lane >= 8 * b) & (lane < 8 * b + 8)
        r = jnp.where(inside, jnp.where(lane == sub + 8 * b, 1.0, 0.0), r)
        diag = jnp.ones((8, n), jnp.float32)
        for j in range(8):
            d = jnp.broadcast_to(cols[j][j : j + 1, :], (8, n))
            diag = jnp.where(sub == j, d, diag)
            if j < 7:
                q = pl.reciprocal(d, approx=True)
                q = q * (2.0 - d * q)
                m = jnp.where(sub > j, cols[j] * q, 0.0)
                for c in range(j + 1, 8):
                    cols[c] = cols[c] - m * jnp.broadcast_to(cols[c][j : j + 1, :], (8, n))
                r = r - m * jnp.broadcast_to(r[j : j + 1, :], (8, n))
        s = lax.rsqrt(diag)
        s = s * (1.5 - 0.5 * diag * s * s)
        r = r * s
        rows[b] = r
        if b < groups - 1:
            p = rank_update(r)
            for i in range(b + 1, groups):
                rows[i] = jnp.where(inside, 0.0, rows[i]) - p[8 * i : 8 * i + 8, :]
    kept = [jnp.where(lane <= sub + 8 * b, rows[b], 0.0) for b in range(groups)]
    return jnp.concatenate(kept, 0)


def times_transposed(a, b):
    return lax.dot_general(
        a, b, (((1,), (1,)), ((), ())), precision=HI, preferred_element_type=jnp.float32
    )


def factor_kernel(a_ref, o_ref):
    n = a_ref.shape[0]
    steps = n // NB
    o_ref[...] = a_ref[...]
    for kb in range(steps):
        own = slice(kb * NB, kb * NB + NB)
        w = inverse_of_factor(o_ref[own, own])
        o_ref[own, own] = w
        if kb == steps - 1:
            break
        lo = (kb + 1) * NB
        o_ref[lo:, own] = times_transposed(o_ref[lo:, own], w)
        for j in range(kb + 1, steps):
            cj = slice(j * NB, j * NB + NB)
            o_ref[j * NB :, cj] = o_ref[j * NB :, cj] - times_transposed(
                o_ref[j * NB :, own], o_ref[cj, own]
            )


def factored(block):
    vmem = pl.BlockSpec(memory_space=pltpu.VMEM)
    n = block.shape[0]
    return pl.pallas_call(
        factor_kernel,
        out_shape=jax.ShapeDtypeStruct(block.shape, jnp.float32),
        in_specs=[vmem],
        out_specs=vmem,
        cost_estimate=pl.CostEstimate(flops=40 * n**3, bytes_accessed=8 * n * n, transcendentals=0),
        name="factor",
    )(block)


def solve_kernel(g_ref, f_ref, o_ref):
    n = f_ref.shape[0]
    o_ref[...] = g_ref[...]
    for kb in range(n // NB):
        own = slice(kb * NB, kb * NB + NB)
        x = times_transposed(o_ref[:, own], f_ref[own, own])
        o_ref[:, own] = x
        lo = (kb + 1) * NB
        if lo < n:
            o_ref[:, lo:] = o_ref[:, lo:] - times_transposed(x, f_ref[lo:, own])


def solved(rows, factor):
    vmem = pl.BlockSpec(memory_space=pltpu.VMEM)
    return pl.pallas_call(
        solve_kernel,
        out_shape=jax.ShapeDtypeStruct(rows.shape, jnp.float32),
        in_specs=[vmem, vmem],
        out_specs=vmem,
        name="solve",
    )(rows, factor)


MESH_IDS = pl.DeviceIdType.MESH
Z, X, Y, GROUPS = 8, 4, 4, 8


def here():
    samp, z, x = lax.axis_index("samp"), lax.axis_index("z"), lax.axis_index("x")
    return samp, z, x


def wrapped(value, size):
    return lax.rem(value + size, size)


def meet(peers):
    barrier = pltpu.get_barrier_semaphore()
    for peer in peers:
        pl.semaphore_signal(barrier, inc=1, device_id=peer, device_id_type=MESH_IDS)
    pl.semaphore_wait(barrier, len(peers))


def at(samp, z, x):
    return {"samp": samp, "z": z, "x": x}


def plane_peers(samp, z, x):
    return [
        (ds, dx, at(wrapped(samp + ds, GROUPS), z, wrapped(x + dx, X)))
        for ds in range(GROUPS)
        for dx in range(X)
        if (ds, dx) != (0, 0)
    ]


def column_peers(samp, z, x):
    return [(dz, at(samp, wrapped(z + dz, Z), x)) for dz in range(1, Z)]


def copy_to(src, dst, send, recv, peer):
    return pltpu.make_async_remote_copy(
        src_ref=src, dst_ref=dst, send_sem=send, recv_sem=recv,
        device_id=peer, device_id_type=MESH_IDS,
    )


def pivots_kernel(mine_ref, slot_ref, out_ref, slots_ref, own_sem, send, recv, zs, zr, ps, pr):
    samp, z, x = here()
    right, left = wrapped(z + 1, Z), wrapped(z - 1, Z)
    column, plane = column_peers(samp, z, x), plane_peers(samp, z, x)
    meet([peer for _, peer in column] + [peer for _, _, peer in plane])
    half = mine_ref.shape[0] // 2

    sends = []
    slots_ref[samp, z, x] = slot_ref[...]
    for dz, peer in column:
        sends.append(copy_to(slot_ref, slots_ref.at[samp, z, x], zs.at[dz], zr.at[dz], peer))
        sends[-1].start()

    own = pltpu.make_async_copy(mine_ref, out_ref.at[z], own_sem)
    own.start()

    def piece(owner, h):
        return out_ref.at[owner, pl.ds(h * half, half)]

    def arrival(d, s, h):
        owner = wrapped(z - 1 - s, Z) if d == 0 else wrapped(z + 1 + s, Z)
        ref = piece(owner, h)
        return copy_to(ref, ref, send.at[d, s, h], recv.at[d, s, h], at(samp, z, x))

    for s in range(4):
        for h in range(2):
            for d in range(2):
                if s == 3 and h != d:
                    continue
                owner = wrapped(z - s, Z) if d == 0 else wrapped(z + s, Z)
                if s > 0:
                    arrival(d, s - 1, h).wait_recv()
                source = mine_ref.at[pl.ds(h * half, half)] if s == 0 else piece(owner, h)
                sends.append(
                    copy_to(source, piece(owner, h), send.at[d, s, h], recv.at[d, s, h],
                            at(samp, right if d == 0 else left, x))
                )
                sends[-1].start()
        if s == 0:
            for dz, _ in column:
                ref = slots_ref.at[samp, wrapped(z - dz, Z), x]
                copy_to(ref, ref, zs.at[dz], zr.at[dz], at(samp, z, x)).wait_recv()
            for ds, dx, peer in plane:
                ref = slots_ref.at[samp, :, x]
                sends.append(copy_to(ref, ref, ps.at[ds, dx], pr.at[ds, dx], peer))
                sends[-1].start()
    for d in range(2):
        for h in range(2):
            for s in range(4):
                if s == 3 and h == d or s == 2 and h != d:
                    arrival(d, s, h).wait_recv()
    for ds, dx, _ in plane:
        ref = slots_ref.at[wrapped(samp - ds, GROUPS), :, wrapped(x - dx, X)]
        copy_to(ref, ref, ps.at[ds, dx], pr.at[ds, dx], at(samp, z, x)).wait_recv()
    for copy in sends:
        copy.wait_send()
    own.wait()


def gathered_pivots(mine, slots):
    vmem = pl.BlockSpec(memory_space=pltpu.VMEM)
    dma = pltpu.SemaphoreType.DMA
    band, width = mine.shape
    return pl.pallas_call(
        pivots_kernel,
        out_shape=(
            jax.ShapeDtypeStruct((Z, band, width), mine.dtype),
            jax.ShapeDtypeStruct((GROUPS, Z, X, 1, 128), slots.dtype),
        ),
        in_specs=[vmem, vmem],
        out_specs=(vmem, vmem),
        scratch_shapes=[dma, dma((2, 4, 2)), dma((2, 4, 2)), dma((Z,)), dma((Z,)),
                        dma((GROUPS, X)), dma((GROUPS, X))],
        compiler_params=pltpu.CompilerParams(collective_id=0, has_side_effects=True),
        name="gather_pivots",
    )(mine, slots)


def rows_kernel(c_ref, o_ref, sib, acc, first0, first1, acc0, acc1, second0, second1,
                ss, sr, s0, r0, s1, r1, t0, q0, t1, q1):
    samp, z, x = here()
    y, core = samp // 2, lax.rem(samp, 2)
    sibling = at(2 * y + 1 - core, z, x)
    ring_y = [(d, wrapped(y + d, Y)) for d in range(1, Y)]
    ring_x = [(d, wrapped(x + d, X)) for d in range(1, X)]
    to_y = [at(2 * v + core, z, x) for _, v in ring_y]
    to_x = [at(samp, z, v) for _, v in ring_x]
    meet([sibling] + to_y + to_x)
    wide = c_ref.shape[4] // 2
    low, high = pl.ds(0, wide), pl.ds(wide, wide)
    sends = []

    def start(copy):
        copy.start()
        sends.append(copy)

    order = (2, 1, 3, 0)
    for d in order:
        v = wrapped(y + d, Y)
        start(copy_to(c_ref.at[v, 1 - core], sib.at[v], ss.at[d], sr.at[d], sibling))
    for d in order:
        v = wrapped(y + d, Y)
        copy_to(sib.at[v], sib.at[v], ss.at[d], sr.at[d], sibling).wait_recv()
        acc[v] = c_ref[v, core] + sib[v]
        if d:
            start(copy_to(acc.at[v, :, :, low], first0.at[d], s0.at[d], r0.at[d],
                          at(2 * v + core, z, x)))
    for d in (2, 1, 3):
        u = wrapped(x + d, X)
        start(copy_to(acc.at[:, u, :, high], first1.at[d], s1.at[d], r1.at[d], at(samp, z, u)))
    me = at(samp, z, x)
    for d in (1, 2, 3):
        copy_to(first0.at[d], first0.at[d], s0.at[d], r0.at[d], me).wait_recv()
    acc0[...] = acc[y, :, :, low] + first0[1] + first0[2] + first0[3]
    for d in (2, 1, 3):
        u = wrapped(x + d, X)
        start(copy_to(acc0.at[u], second0.at[d], t0.at[d], q0.at[d], at(samp, z, u)))
    for d in (1, 2, 3):
        copy_to(first1.at[d], first1.at[d], s1.at[d], r1.at[d], me).wait_recv()
    acc1[...] = acc[:, x, :, high] + first1[1] + first1[2] + first1[3]
    for d in (2, 1, 3):
        v = wrapped(y + d, Y)
        start(copy_to(acc1.at[v], second1.at[d], t1.at[d], q1.at[d], at(2 * v + core, z, x)))
    for d in (1, 2, 3):
        copy_to(second0.at[d], second0.at[d], t0.at[d], q0.at[d], me).wait_recv()
    o_ref[:, low] = acc0[x] + second0[1] + second0[2] + second0[3]
    for d in (1, 2, 3):
        copy_to(second1.at[d], second1.at[d], t1.at[d], q1.at[d], me).wait_recv()
    o_ref[:, high] = acc1[y] + second1[1] + second1[2] + second1[3]
    for copy in sends:
        copy.wait_send()


def summed_rows(partial):
    vmem = pl.BlockSpec(memory_space=pltpu.VMEM)
    dma = pltpu.SemaphoreType.DMA
    n = partial.shape[1]
    rows = partial.shape[0] // (GROUPS * X)
    wide = n // 2
    f32 = jnp.float32
    return pl.pallas_call(
        rows_kernel,
        out_shape=jax.ShapeDtypeStruct((rows, n), f32),
        in_specs=[vmem],
        out_specs=vmem,
        scratch_shapes=[
            pltpu.VMEM((Y, X, rows, n), f32), pltpu.VMEM((Y, X, rows, n), f32),
            pltpu.VMEM((Y, X, rows, wide), f32), pltpu.VMEM((X, Y, rows, wide), f32),
            pltpu.VMEM((X, rows, wide), f32), pltpu.VMEM((Y, rows, wide), f32),
            pltpu.VMEM((X, rows, wide), f32), pltpu.VMEM((Y, rows, wide), f32),
        ] + [dma((4,))] * 10,
        compiler_params=pltpu.CompilerParams(collective_id=1, has_side_effects=True),
        name="sum_rows",
    )(partial.reshape(Y, 2, X, rows, n))


def block_kernel(p_ref, o_ref, got, piece, ps, pr, zs, zr, xs, xr, ys, yr, ys2, yr2, xs2, xr2, cs, cr):
    samp, z, x = here()
    y, core = samp // 2, lax.rem(samp, 2)
    xh, xl = x // 2, lax.rem(x, 2)
    sibling = at(2 * y + 1 - core, z, x)
    column, plane = column_peers(samp, z, x), plane_peers(samp, z, x)
    meet([peer for _, peer in column] + [peer for _, _, peer in plane])
    me = at(samp, z, x)
    wide = p_ref.shape[4] // 2
    sends = []

    def start(copy):
        copy.start()
        sends.append(copy)

    def cols(xlow, color=None):
        if color is None:
            return pl.ds(pl.multiple_of(xlow * wide, wide), wide)
        return pl.ds(pl.multiple_of(xlow * wide + color * (wide // 2), wide // 2), wide // 2)

    def arrived(ref, send, recv):
        copy_to(ref, ref, send, recv, me).wait_recv()

    for ds, dx, peer in plane:
        s, u = wrapped(samp + ds, GROUPS), wrapped(x + dx, X)
        start(copy_to(p_ref.at[s // 2, lax.rem(s, 2), u // 2, :, cols(lax.rem(u, 2))],
                      got.at[ds, dx], ps.at[ds, dx], pr.at[ds, dx], peer))
    total = p_ref[y, core, xh, :, cols(xl)]
    for ds, dx, _ in plane:
        arrived(got.at[ds, dx], ps.at[ds, dx], pr.at[ds, dx])
    for ds, dx, _ in plane:
        total = total + got[ds, dx]
    piece[...] = total
    o_ref[z, y, core, xh, :, cols(xl)] = total
    for dz, peer in column:
        start(copy_to(piece, o_ref.at[z, y, core, xh, :, cols(xl)], zs.at[dz], zr.at[dz], peer))
    for dz, _ in column:
        arrived(o_ref.at[wrapped(z - dz, Z), y, core, xh, :, cols(xl)], zs.at[dz], zr.at[dz])
    for d in (2, 1, 3):
        v, u = wrapped(y + d, Y), wrapped(x + d, X)
        ref0 = o_ref.at[:, y, core, xh, :, cols(xl, 0)]
        start(copy_to(ref0, ref0, xs.at[d], xr.at[d], at(samp, z, u)))
        ref1 = o_ref.at[:, y, core, xh, :, cols(xl, 1)]
        start(copy_to(ref1, ref1, ys.at[d], yr.at[d], at(2 * v + core, z, x)))
    for d in (1, 2, 3):
        u = wrapped(x - d, X)
        arrived(o_ref.at[:, y, core, u // 2, :, cols(lax.rem(u, 2), 0)], xs.at[d], xr.at[d])
    for d in (2, 1, 3):
        v = wrapped(y + d, Y)
        for low in range(2):
            ref = o_ref.at[:, y, core, :, :, cols(low, 0)]
            start(copy_to(ref, ref, ys2.at[d, low], yr2.at[d, low], at(2 * v + core, z, x)))
    for d in (1, 2, 3):
        v = wrapped(y - d, Y)
        arrived(o_ref.at[:, v, core, xh, :, cols(xl, 1)], ys.at[d], yr.at[d])
    for d in (2, 1, 3):
        u = wrapped(x + d, X)
        ref = o_ref.at[:, :, core, xh, :, cols(xl, 1)]
        start(copy_to(ref, ref, xs2.at[d], xr2.at[d], at(samp, z, u)))
    for d in (1, 3, 2):
        v = wrapped(y - d, Y)
        for low in range(2):
            arrived(o_ref.at[:, v, core, :, :, cols(low, 0)], ys2.at[d, low], yr2.at[d, low])
    for d in (1, 3, 2):
        u = wrapped(x - d, X)
        arrived(o_ref.at[:, :, core, u // 2, :, cols(lax.rem(u, 2), 1)], xs2.at[d], xr2.at[d])
    for v in range(Y):
        ref = o_ref.at[:, v, core]
        start(copy_to(ref, ref, cs.at[v], cr.at[v], sibling))
    for v in range(Y):
        arrived(o_ref.at[:, v, 1 - core], cs.at[v], cr.at[v])
    for copy in sends:
        copy.wait_send()


def summed_block(part):
    vmem = pl.BlockSpec(memory_space=pltpu.VMEM)
    dma = pltpu.SemaphoreType.DMA
    band, n = part.shape
    f32 = jnp.float32
    out = pl.pallas_call(
        block_kernel,
        out_shape=jax.ShapeDtypeStruct((Z, Y, 2, 2, 8, n), f32),
        in_specs=[vmem],
        out_specs=vmem,
        scratch_shapes=[
            pltpu.VMEM((GROUPS, X, 8, n // 2), f32), pltpu.VMEM((8, n // 2), f32),
            dma((GROUPS, X)), dma((GROUPS, X)), dma((Z,)), dma((Z,)),
            dma((4,)), dma((4,)), dma((4,)), dma((4,)),
            dma((4, 2)), dma((4, 2)), dma((4,)), dma((4,)), dma((4,)), dma((4,)),
        ],
        compiler_params=pltpu.CompilerParams(collective_id=2, has_side_effects=True),
        name="sum_block",
    )(part.reshape(Y, 2, 2, 8, n))
    return out.reshape(Z * band, n)


def on_device(jacobian, sample_slot, panel_index, shift_value):
    width = sample_slot.shape[0]
    group_width = width * lax.axis_size(PAR)
    samples = group_width * lax.axis_size("samp")
    pivot_group = panel_index[0] // group_width
    rotation = panel_index[0] % group_width
    tile = lax.all_to_all(jacobian, PLANE, split_axis=1, concat_axis=0, tiled=True)
    band = group_width // lax.axis_size("z")
    mine = lax.dynamic_slice_in_dim(tile, pivot_group * band, band, 0)
    padded = jnp.pad(sample_slot, (0, 128 - width)).reshape(1, 128)
    raw, slots = gathered_pivots(mine, padded)
    raw = raw.reshape(group_width, -1)
    slots = slots[..., 0, :width].reshape(-1, group_width)
    own_slots = lax.dynamic_index_in_dim(slots, lax.axis_index("samp"), 0, keepdims=False)
    pivot_slots = lax.dynamic_index_in_dim(slots, pivot_group, 0, keepdims=False)
    column = jnp.arange(group_width, dtype=jnp.int32)
    chosen = (pivot_slots[None, :] == ((column + rotation) % group_width)[:, None]).astype(jnp.bfloat16)

    pivot = lax.dot_general(
        chosen, raw, (((1,), (0,)), ((), ())), preferred_element_type=jnp.float32
    ).astype(jnp.bfloat16)

    contract = (((1,), (1,)), ((), ()))
    part = lax.dynamic_slice_in_dim(pivot, lax.axis_index("z") * band, band, 0)
    pivot_part = lax.dot_general(part, pivot, contract, preferred_element_type=jnp.float32)
    partial = lax.dot_general(tile, pivot, contract, preferred_element_type=jnp.float32)
    rows = summed_rows(partial)
    group_rows = lax.all_gather(rows, PAR, axis=0, tiled=True)
    block = summed_block(pivot_part)
    identity_matrix = jnp.eye(group_width, dtype=jnp.float32)
    block = block / samples + shift_value[0] * identity_matrix

    position = lax.axis_index(PAR) * width + jnp.arange(width, dtype=jnp.int32)
    hit = own_slots[None, :] == position[:, None]
    source = jnp.sum(jnp.where(hit, column[None, :], 0), axis=1)
    my_rows = jnp.take(group_rows, source, axis=0) / samples
    on_pivot = lax.axis_index("samp") == pivot_group
    shifted = position[:, None] == ((column + rotation) % group_width)[None, :]
    my_rows = my_rows + jnp.where(shifted & on_pivot, shift_value[0], 0.0)
    return solved(my_rows, factored(block))


def solution(mesh):
    torus = Mesh(mesh.devices.reshape(mesh.shape["samp"], 8, 4), ("samp", "z", "x"))
    return jax.shard_map(
        on_device,
        mesh=torus,
        in_specs=(P(ALL, None), P(ALL), P(), P()),
        out_specs=P(ALL, None),
        check_vma=False,
    )
```

```python
import jax
import jax.numpy as jnp
from jax import lax
from jax.experimental import pallas as pl
from jax.experimental.pallas import tpu as pltpu
from jax.sharding import Mesh
from jax.sharding import PartitionSpec as P

PAR = ("z", "x")
PLANE = ("samp", "x")
ALL = ("samp", "z", "x")
NB = 128
HI = lax.Precision.HIGHEST


def rank_update(r):
    h = r.astype(jnp.bfloat16).astype(jnp.float32)
    m = (r - h).astype(jnp.bfloat16).astype(jnp.float32)
    l = (r - h - m).astype(jnp.bfloat16).astype(jnp.float32)
    lhs = jnp.concatenate([h, h, m, h, l, m], 0).astype(jnp.bfloat16)
    rhs = jnp.concatenate([h, m, h, l, h, m], 0).astype(jnp.bfloat16)
    return lax.dot_general(
        lhs, rhs, (((0,), (0,)), ((), ())), preferred_element_type=jnp.float32
    )


def inverse_of_factor(block):
    n = block.shape[0]
    groups = n // 8
    rows = [block[8 * i : 8 * i + 8, :] for i in range(groups)]
    sub = lax.broadcasted_iota(jnp.int32, (8, n), 0)
    lane = lax.broadcasted_iota(jnp.int32, (8, n), 1)
    for b in range(groups):
        r = rows[b]
        cols = [jnp.broadcast_to(r[:, 8 * b + j : 8 * b + j + 1], (8, n)) for j in range(8)]
        inside = (lane >= 8 * b) & (lane < 8 * b + 8)
        r = jnp.where(inside, jnp.where(lane == sub + 8 * b, 1.0, 0.0), r)
        diag = jnp.ones((8, n), jnp.float32)
        for j in range(8):
            d = jnp.broadcast_to(cols[j][j : j + 1, :], (8, n))
            diag = jnp.where(sub == j, d, diag)
            if j < 7:
                q = pl.reciprocal(d, approx=True)
                q = q * (2.0 - d * q)
                m = jnp.where(sub > j, cols[j] * q, 0.0)
                for c in range(j + 1, 8):
                    cols[c] = cols[c] - m * jnp.broadcast_to(cols[c][j : j + 1, :], (8, n))
                r = r - m * jnp.broadcast_to(r[j : j + 1, :], (8, n))
        s = lax.rsqrt(diag)
        s = s * (1.5 - 0.5 * diag * s * s)
        r = r * s
        rows[b] = r
        if b < groups - 1:
            p = rank_update(r)
            for i in range(b + 1, groups):
                rows[i] = jnp.where(inside, 0.0, rows[i]) - p[8 * i : 8 * i + 8, :]
    kept = [jnp.where(lane <= sub + 8 * b, rows[b], 0.0) for b in range(groups)]
    return jnp.concatenate(kept, 0)


def times_transposed(a, b):
    return lax.dot_general(
        a, b, (((1,), (1,)), ((), ())), precision=HI, preferred_element_type=jnp.float32
    )


def factor_kernel(a_ref, o_ref):
    n = a_ref.shape[0]
    steps = n // NB
    o_ref[...] = a_ref[...]
    for kb in range(steps):
        own = slice(kb * NB, kb * NB + NB)
        w = inverse_of_factor(o_ref[own, own])
        o_ref[own, own] = w
        if kb == steps - 1:
            break
        lo = (kb + 1) * NB
        o_ref[lo:, own] = times_transposed(o_ref[lo:, own], w)
        for j in range(kb + 1, steps):
            cj = slice(j * NB, j * NB + NB)
            o_ref[j * NB :, cj] = o_ref[j * NB :, cj] - times_transposed(
                o_ref[j * NB :, own], o_ref[cj, own]
            )


def factored(block):
    vmem = pl.BlockSpec(memory_space=pltpu.VMEM)
    n = block.shape[0]
    return pl.pallas_call(
        factor_kernel,
        out_shape=jax.ShapeDtypeStruct(block.shape, jnp.float32),
        in_specs=[vmem],
        out_specs=vmem,
        cost_estimate=pl.CostEstimate(flops=40 * n**3, bytes_accessed=8 * n * n, transcendentals=0),
        name="factor",
    )(block)


def solve_kernel(g_ref, f_ref, o_ref):
    n = f_ref.shape[0]
    o_ref[...] = g_ref[...]
    for kb in range(n // NB):
        own = slice(kb * NB, kb * NB + NB)
        x = times_transposed(o_ref[:, own], f_ref[own, own])
        o_ref[:, own] = x
        lo = (kb + 1) * NB
        if lo < n:
            o_ref[:, lo:] = o_ref[:, lo:] - times_transposed(x, f_ref[lo:, own])


def solved(rows, factor):
    vmem = pl.BlockSpec(memory_space=pltpu.VMEM)
    return pl.pallas_call(
        solve_kernel,
        out_shape=jax.ShapeDtypeStruct(rows.shape, jnp.float32),
        in_specs=[vmem, vmem],
        out_specs=vmem,
        name="solve",
    )(rows, factor)


MESH_IDS = pl.DeviceIdType.MESH
Z, X, Y, GROUPS = 8, 4, 4, 8
CHUNKS = 4


def here():
    samp, z, x = lax.axis_index("samp"), lax.axis_index("z"), lax.axis_index("x")
    return samp, z, x


def wrapped(value, size):
    return lax.rem(value + size, size)


def meet(peers):
    barrier = pltpu.get_barrier_semaphore()
    for peer in peers:
        pl.semaphore_signal(barrier, inc=1, device_id=peer, device_id_type=MESH_IDS)
    pl.semaphore_wait(barrier, len(peers))


def at(samp, z, x):
    return {"samp": samp, "z": z, "x": x}


def plane_peers(samp, z, x):
    return [
        (ds, dx, at(wrapped(samp + ds, GROUPS), z, wrapped(x + dx, X)))
        for ds in range(GROUPS)
        for dx in range(X)
        if (ds, dx) != (0, 0)
    ]


def column_peers(samp, z, x):
    return [(dz, at(samp, wrapped(z + dz, Z), x)) for dz in range(1, Z)]


def copy_to(src, dst, send, recv, peer):
    return pltpu.make_async_remote_copy(
        src_ref=src, dst_ref=dst, send_sem=send, recv_sem=recv,
        device_id=peer, device_id_type=MESH_IDS,
    )


def exchange_kernel(jac_ref, slot_ref, group_ref, tile_ref, pivot_ref, slots_ref,
                    own_sem, send, recv, zsend, zrecv, ps, pr, zs, zr):
    samp, z, x = here()
    right, left = wrapped(z + 1, Z), wrapped(z - 1, Z)
    column, plane = column_peers(samp, z, x), plane_peers(samp, z, x)
    me = at(samp, z, x)
    meet([peer for _, peer in column] + [peer for _, _, peer in plane])
    rows = jac_ref.shape[0]
    tile = tile_ref.shape[-1]
    wide = tile // CHUNKS
    sends = []

    def start(copy):
        copy.start()
        sends.append(copy)

    def arrived(ref, send_sem, recv_sem):
        copy_to(ref, ref, send_sem, recv_sem, me).wait_recv()

    def cols(q):
        return pl.ds(q * wide, wide)

    slots_ref[samp, z, x] = slot_ref[...]
    for ds, dx, peer in plane:
        start(copy_to(slot_ref, slots_ref.at[samp, z, x], ps.at[ds, dx], pr.at[ds, dx], peer))

    owns = []
    for q in range(CHUNKS):
        for ds, dx, peer in plane:
            s, u = wrapped(samp + ds, GROUPS), wrapped(x + dx, X)
            first = pl.multiple_of((s * X + u) * tile + q * wide, wide)
            start(copy_to(jac_ref.at[:, pl.ds(first, wide)], tile_ref.at[samp, x, :, cols(q)],
                          send.at[q, ds, dx], recv.at[q, ds, dx], peer))
        first = pl.multiple_of((samp * X + x) * tile + q * wide, wide)
        owns.append(pltpu.make_async_copy(jac_ref.at[:, pl.ds(first, wide)],
                                          tile_ref.at[samp, x, :, cols(q)], own_sem.at[q]))
        owns[-1].start()

    for ds, dx, _ in plane:
        arrived(slots_ref.at[wrapped(samp - ds, GROUPS), z, wrapped(x - dx, X)],
                ps.at[ds, dx], pr.at[ds, dx])
    for dz, peer in column:
        ref = slots_ref.at[:, z]
        start(copy_to(ref, ref, zs.at[dz], zr.at[dz], peer))

    def hop(d, s, q):
        owner = wrapped(z - s, Z) if d == 0 else wrapped(z + s, Z)
        ref = pivot_ref.at[owner, :, :, cols(q)]
        start(copy_to(ref, ref, zsend.at[d, s, q], zrecv.at[d, s, q],
                      at(samp, right if d == 0 else left, x)))

    def came(d, s, q):
        owner = wrapped(z - 1 - s, Z) if d == 0 else wrapped(z + 1 + s, Z)
        arrived(pivot_ref.at[owner, :, :, cols(q)], zsend.at[d, s, q], zrecv.at[d, s, q])

    def farthest(d, q):
        return d == q % 2

    def forward(q):
        for s in range(1, 4):
            for d in range(2):
                came(d, s - 1, q)
                if s < 3 or farthest(d, q):
                    hop(d, s, q)

    for q in range(CHUNKS):
        for ds, dx, _ in plane:
            arrived(tile_ref.at[wrapped(samp - ds, GROUPS), wrapped(x - dx, X), :, cols(q)],
                    send.at[q, ds, dx], recv.at[q, ds, dx])
        owns[q].wait()
        picked = tile_ref[0, :, :, cols(q)]
        for g in range(1, GROUPS):
            picked = jnp.where(group_ref[0] == g, tile_ref[g, :, :, cols(q)], picked)
        pivot_ref[z, :, :, cols(q)] = picked
        for d in range(2):
            hop(d, 0, q)
        if q > 0:
            forward(q - 1)
    forward(CHUNKS - 1)
    for q in range(CHUNKS):
        came(0 if farthest(0, q) else 1, 3, q)
    for dz, _ in column:
        arrived(slots_ref.at[:, wrapped(z - dz, Z)], zs.at[dz], zr.at[dz])
    for copy in sends:
        copy.wait_send()


def exchanged(jacobian, slots, group):
    vmem = pl.BlockSpec(memory_space=pltpu.VMEM)
    dma = pltpu.SemaphoreType.DMA
    rows, params = jacobian.shape
    tile = params // (GROUPS * X)
    return pl.pallas_call(
        exchange_kernel,
        out_shape=(
            jax.ShapeDtypeStruct((GROUPS, X, rows, tile), jacobian.dtype),
            jax.ShapeDtypeStruct((Z, X, rows, tile), jacobian.dtype),
            jax.ShapeDtypeStruct((GROUPS, Z, X, 1, 128), slots.dtype),
        ),
        in_specs=[pl.BlockSpec(memory_space=pl.ANY), vmem,
                  pl.BlockSpec(memory_space=pltpu.SMEM)],
        out_specs=(vmem, vmem, vmem),
        scratch_shapes=[dma((CHUNKS,)), dma((CHUNKS, GROUPS, X)), dma((CHUNKS, GROUPS, X)),
                        dma((2, 4, CHUNKS)), dma((2, 4, CHUNKS)),
                        dma((GROUPS, X)), dma((GROUPS, X)), dma((Z,)), dma((Z,))],
        compiler_params=pltpu.CompilerParams(collective_id=0, has_side_effects=True),
        name="exchange",
    )(jacobian, slots, group)


def rows_kernel(c_ref, o_ref, sib, acc, first0, first1, acc0, acc1, second0, second1,
                ss, sr, s0, r0, s1, r1, t0, q0, t1, q1):
    samp, z, x = here()
    y, core = samp // 2, lax.rem(samp, 2)
    sibling = at(2 * y + 1 - core, z, x)
    ring_y = [(d, wrapped(y + d, Y)) for d in range(1, Y)]
    ring_x = [(d, wrapped(x + d, X)) for d in range(1, X)]
    to_y = [at(2 * v + core, z, x) for _, v in ring_y]
    to_x = [at(samp, z, v) for _, v in ring_x]
    meet([sibling] + to_y + to_x)
    wide = c_ref.shape[4] // 2
    low, high = pl.ds(0, wide), pl.ds(wide, wide)
    sends = []

    def start(copy):
        copy.start()
        sends.append(copy)

    order = (2, 1, 3, 0)
    for d in order:
        v = wrapped(y + d, Y)
        start(copy_to(c_ref.at[v, 1 - core], sib.at[v], ss.at[d], sr.at[d], sibling))
    for d in order:
        v = wrapped(y + d, Y)
        copy_to(sib.at[v], sib.at[v], ss.at[d], sr.at[d], sibling).wait_recv()
        acc[v] = c_ref[v, core] + sib[v]
        if d:
            start(copy_to(acc.at[v, :, :, low], first0.at[d], s0.at[d], r0.at[d],
                          at(2 * v + core, z, x)))
    for d in (2, 1, 3):
        u = wrapped(x + d, X)
        start(copy_to(acc.at[:, u, :, high], first1.at[d], s1.at[d], r1.at[d], at(samp, z, u)))
    me = at(samp, z, x)
    for d in (1, 2, 3):
        copy_to(first0.at[d], first0.at[d], s0.at[d], r0.at[d], me).wait_recv()
    acc0[...] = acc[y, :, :, low] + first0[1] + first0[2] + first0[3]
    for d in (2, 1, 3):
        u = wrapped(x + d, X)
        start(copy_to(acc0.at[u], second0.at[d], t0.at[d], q0.at[d], at(samp, z, u)))
    for d in (1, 2, 3):
        copy_to(first1.at[d], first1.at[d], s1.at[d], r1.at[d], me).wait_recv()
    acc1[...] = acc[:, x, :, high] + first1[1] + first1[2] + first1[3]
    for d in (2, 1, 3):
        v = wrapped(y + d, Y)
        start(copy_to(acc1.at[v], second1.at[d], t1.at[d], q1.at[d], at(2 * v + core, z, x)))
    for d in (1, 2, 3):
        copy_to(second0.at[d], second0.at[d], t0.at[d], q0.at[d], me).wait_recv()
    o_ref[:, low] = acc0[x] + second0[1] + second0[2] + second0[3]
    for d in (1, 2, 3):
        copy_to(second1.at[d], second1.at[d], t1.at[d], q1.at[d], me).wait_recv()
    o_ref[:, high] = acc1[y] + second1[1] + second1[2] + second1[3]
    for copy in sends:
        copy.wait_send()


def summed_rows(partial):
    vmem = pl.BlockSpec(memory_space=pltpu.VMEM)
    dma = pltpu.SemaphoreType.DMA
    n = partial.shape[1]
    rows = partial.shape[0] // (GROUPS * X)
    wide = n // 2
    f32 = jnp.float32
    return pl.pallas_call(
        rows_kernel,
        out_shape=jax.ShapeDtypeStruct((rows, n), f32),
        in_specs=[vmem],
        out_specs=vmem,
        scratch_shapes=[
            pltpu.VMEM((Y, X, rows, n), f32), pltpu.VMEM((Y, X, rows, n), f32),
            pltpu.VMEM((Y, X, rows, wide), f32), pltpu.VMEM((X, Y, rows, wide), f32),
            pltpu.VMEM((X, rows, wide), f32), pltpu.VMEM((Y, rows, wide), f32),
            pltpu.VMEM((X, rows, wide), f32), pltpu.VMEM((Y, rows, wide), f32),
        ] + [dma((4,))] * 10,
        compiler_params=pltpu.CompilerParams(collective_id=1, has_side_effects=True),
        name="sum_rows",
    )(partial.reshape(Y, 2, X, rows, n))


def block_kernel(p_ref, o_ref, got, piece, ps, pr, zs, zr, xs, xr, ys, yr, ys2, yr2, xs2, xr2, cs, cr):
    samp, z, x = here()
    y, core = samp // 2, lax.rem(samp, 2)
    xh, xl = x // 2, lax.rem(x, 2)
    sibling = at(2 * y + 1 - core, z, x)
    column, plane = column_peers(samp, z, x), plane_peers(samp, z, x)
    meet([peer for _, peer in column] + [peer for _, _, peer in plane])
    me = at(samp, z, x)
    wide = p_ref.shape[4] // 2
    sends = []

    def start(copy):
        copy.start()
        sends.append(copy)

    def cols(xlow, color=None):
        if color is None:
            return pl.ds(pl.multiple_of(xlow * wide, wide), wide)
        return pl.ds(pl.multiple_of(xlow * wide + color * (wide // 2), wide // 2), wide // 2)

    def arrived(ref, send, recv):
        copy_to(ref, ref, send, recv, me).wait_recv()

    for ds, dx, peer in plane:
        s, u = wrapped(samp + ds, GROUPS), wrapped(x + dx, X)
        start(copy_to(p_ref.at[s // 2, lax.rem(s, 2), u // 2, :, cols(lax.rem(u, 2))],
                      got.at[ds, dx], ps.at[ds, dx], pr.at[ds, dx], peer))
    total = p_ref[y, core, xh, :, cols(xl)]
    for ds, dx, _ in plane:
        arrived(got.at[ds, dx], ps.at[ds, dx], pr.at[ds, dx])
    for ds, dx, _ in plane:
        total = total + got[ds, dx]
    piece[...] = total
    o_ref[z, y, core, xh, :, cols(xl)] = total
    for dz, peer in column:
        start(copy_to(piece, o_ref.at[z, y, core, xh, :, cols(xl)], zs.at[dz], zr.at[dz], peer))
    for dz, _ in column:
        arrived(o_ref.at[wrapped(z - dz, Z), y, core, xh, :, cols(xl)], zs.at[dz], zr.at[dz])
    for d in (2, 1, 3):
        v, u = wrapped(y + d, Y), wrapped(x + d, X)
        ref0 = o_ref.at[:, y, core, xh, :, cols(xl, 0)]
        start(copy_to(ref0, ref0, xs.at[d], xr.at[d], at(samp, z, u)))
        ref1 = o_ref.at[:, y, core, xh, :, cols(xl, 1)]
        start(copy_to(ref1, ref1, ys.at[d], yr.at[d], at(2 * v + core, z, x)))
    for d in (1, 2, 3):
        u = wrapped(x - d, X)
        arrived(o_ref.at[:, y, core, u // 2, :, cols(lax.rem(u, 2), 0)], xs.at[d], xr.at[d])
    for d in (2, 1, 3):
        v = wrapped(y + d, Y)
        for low in range(2):
            ref = o_ref.at[:, y, core, :, :, cols(low, 0)]
            start(copy_to(ref, ref, ys2.at[d, low], yr2.at[d, low], at(2 * v + core, z, x)))
    for d in (1, 2, 3):
        v = wrapped(y - d, Y)
        arrived(o_ref.at[:, v, core, xh, :, cols(xl, 1)], ys.at[d], yr.at[d])
    for d in (2, 1, 3):
        u = wrapped(x + d, X)
        ref = o_ref.at[:, :, core, xh, :, cols(xl, 1)]
        start(copy_to(ref, ref, xs2.at[d], xr2.at[d], at(samp, z, u)))
    for d in (1, 3, 2):
        v = wrapped(y - d, Y)
        for low in range(2):
            arrived(o_ref.at[:, v, core, :, :, cols(low, 0)], ys2.at[d, low], yr2.at[d, low])
    for d in (1, 3, 2):
        u = wrapped(x - d, X)
        arrived(o_ref.at[:, :, core, u // 2, :, cols(lax.rem(u, 2), 1)], xs2.at[d], xr2.at[d])
    for v in range(Y):
        ref = o_ref.at[:, v, core]
        start(copy_to(ref, ref, cs.at[v], cr.at[v], sibling))
    for v in range(Y):
        arrived(o_ref.at[:, v, 1 - core], cs.at[v], cr.at[v])
    for copy in sends:
        copy.wait_send()


def summed_block(part):
    vmem = pl.BlockSpec(memory_space=pltpu.VMEM)
    dma = pltpu.SemaphoreType.DMA
    band, n = part.shape
    f32 = jnp.float32
    out = pl.pallas_call(
        block_kernel,
        out_shape=jax.ShapeDtypeStruct((Z, Y, 2, 2, 8, n), f32),
        in_specs=[vmem],
        out_specs=vmem,
        scratch_shapes=[
            pltpu.VMEM((GROUPS, X, 8, n // 2), f32), pltpu.VMEM((8, n // 2), f32),
            dma((GROUPS, X)), dma((GROUPS, X)), dma((Z,)), dma((Z,)),
            dma((4,)), dma((4,)), dma((4,)), dma((4,)),
            dma((4, 2)), dma((4, 2)), dma((4,)), dma((4,)), dma((4,)), dma((4,)),
        ],
        compiler_params=pltpu.CompilerParams(collective_id=2, has_side_effects=True),
        name="sum_block",
    )(part.reshape(Y, 2, 2, 8, n))
    return out.reshape(Z * band, n)


def on_device(jacobian, sample_slot, panel_index, shift_value):
    width = sample_slot.shape[0]
    group_width = width * lax.axis_size(PAR)
    samples = group_width * lax.axis_size("samp")
    pivot_group = panel_index[0] // group_width
    rotation = panel_index[0] % group_width
    band = group_width // lax.axis_size("z")
    padded = jnp.pad(sample_slot, (0, 128 - width)).reshape(1, 128)
    tile, raw, slots = exchanged(jacobian, padded, pivot_group.reshape(1))
    tile = tile.reshape(group_width, -1)
    raw = raw.reshape(group_width, -1)
    slots = slots[..., 0, :width].reshape(-1, group_width)
    own_slots = lax.dynamic_index_in_dim(slots, lax.axis_index("samp"), 0, keepdims=False)
    pivot_slots = lax.dynamic_index_in_dim(slots, pivot_group, 0, keepdims=False)
    column = jnp.arange(group_width, dtype=jnp.int32)
    chosen = (pivot_slots[None, :] == ((column + rotation) % group_width)[:, None]).astype(jnp.bfloat16)

    pivot = lax.dot_general(
        chosen, raw, (((1,), (0,)), ((), ())), preferred_element_type=jnp.float32
    ).astype(jnp.bfloat16)

    contract = (((1,), (1,)), ((), ()))
    part = lax.dynamic_slice_in_dim(pivot, lax.axis_index("z") * band, band, 0)
    pivot_part = lax.dot_general(part, pivot, contract, preferred_element_type=jnp.float32)
    partial = lax.dot_general(tile, pivot, contract, preferred_element_type=jnp.float32)
    rows = summed_rows(partial)
    group_rows = lax.all_gather(rows, PAR, axis=0, tiled=True)
    block = summed_block(pivot_part)
    identity_matrix = jnp.eye(group_width, dtype=jnp.float32)
    block = block / samples + shift_value[0] * identity_matrix

    position = lax.axis_index(PAR) * width + jnp.arange(width, dtype=jnp.int32)
    hit = own_slots[None, :] == position[:, None]
    source = jnp.sum(jnp.where(hit, column[None, :], 0), axis=1)
    my_rows = jnp.take(group_rows, source, axis=0) / samples
    on_pivot = lax.axis_index("samp") == pivot_group
    shifted = position[:, None] == ((column + rotation) % group_width)[None, :]
    my_rows = my_rows + jnp.where(shifted & on_pivot, shift_value[0], 0.0)
    return solved(my_rows, factored(block))


def solution(mesh):
    torus = Mesh(mesh.devices.reshape(mesh.shape["samp"], 8, 4), ("samp", "z", "x"))
    return jax.shard_map(
        on_device,
        mesh=torus,
        in_specs=(P(ALL, None), P(ALL), P(), P()),
        out_specs=P(ALL, None),
        check_vma=False,
    )
```

```python
import functools

import jax
import jax.numpy as jnp
from jax import lax
from jax.experimental import pallas as pl
from jax.experimental.pallas import tpu as pltpu
from jax.sharding import Mesh
from jax.sharding import PartitionSpec as P

PAR = ("z", "x")
PLANE = ("samp", "x")
ALL = ("samp", "z", "x")
NB = 128
STEP = 16
HI = lax.Precision.HIGHEST


def rank_update(r):
    h = r.astype(jnp.bfloat16).astype(jnp.float32)
    m = (r - h).astype(jnp.bfloat16).astype(jnp.float32)
    l = (r - h - m).astype(jnp.bfloat16).astype(jnp.float32)
    lhs = jnp.concatenate([h, h, m, h, l, m], 0).astype(jnp.bfloat16)
    rhs = jnp.concatenate([h, m, h, l, h, m], 0).astype(jnp.bfloat16)
    return lax.dot_general(
        lhs, rhs, (((0,), (0,)), ((), ())), preferred_element_type=jnp.float32
    )


def inverse_of_factor(block, filler):
    n = block.shape[0]
    groups = n // STEP
    rows = [block[STEP * i : STEP * i + STEP, :] for i in range(groups)]
    sub = lax.broadcasted_iota(jnp.int32, (STEP, n), 0)
    lane = lax.broadcasted_iota(jnp.int32, (STEP, n), 1)
    for b in range(groups):
        first = STEP * b
        r = rows[b]
        cols = [jnp.broadcast_to(r[:, first + j : first + j + 1], (STEP, n)) for j in range(STEP)]
        inside = (lane >= first) & (lane < first + STEP)
        r = jnp.where(inside, jnp.where(lane == sub + first, 1.0, 0.0), r)
        diag = jnp.ones((STEP, n), jnp.float32)
        for j in range(STEP):
            d = jnp.broadcast_to(cols[j][j : j + 1, :], (8, n))
            diag = jnp.where(sub == j, jnp.concatenate([d] * (STEP // 8), 0), diag)
            if j == STEP - 1:
                break
            low = (j + 1) // 8 * 8
            below = (STEP - low) // 8
            q = pl.reciprocal(d, approx=True)
            e = jnp.concatenate([1.0 - d * q] * below, 0)
            m = jnp.where(sub[low:] > j, cols[j][low:], 0.0) * jnp.concatenate([q] * below, 0)
            m = m + m * e

            def eliminated(v):
                left = v[low:] - m * jnp.broadcast_to(v[j : j + 1, :], (STEP - low, n))
                return left if low == 0 else jnp.concatenate([v[:low], left], 0)

            for c in range(j + 1, STEP):
                cols[c] = eliminated(cols[c])
            r = eliminated(r)
        s = lax.rsqrt(diag)
        s = s * (1.5 - 0.5 * diag * s * s)
        r = r * s
        rows[b] = r
        if b < groups - 1:
            p = rank_update(r)
            for i in range(b + 1, groups):
                rows[i] = jnp.where(inside, 0.0, rows[i]) - p[STEP * i : STEP * i + STEP, :]
        filler()
    kept = [jnp.where(lane <= sub + STEP * b, rows[b], 0.0) for b in range(groups)]
    return jnp.concatenate(kept, 0)


def times_transposed(a, b):
    return lax.dot_general(
        a, b, (((1,), (1,)), ((), ())), precision=HI, preferred_element_type=jnp.float32
    )


def factor(a_ref, o_ref, between):
    n = a_ref.shape[0]
    steps = n // NB
    waiting = []

    def run(count):
        for _ in range(min(count, len(waiting))):
            waiting.pop(0)()

    for kb in range(steps):
        s_ref = a_ref if kb == 0 else o_ref
        own = slice(kb * NB, kb * NB + NB)
        share = -(-len(waiting) // (NB // STEP))
        w = inverse_of_factor(s_ref[own, own], lambda: run(share))
        run(len(waiting))
        o_ref[own, own] = w
        between(kb)
        if kb == steps - 1:
            break
        lo = (kb + 1) * NB
        o_ref[lo:, own] = times_transposed(s_ref[lo:, own], w)

        def update(j, top, end, s_ref=s_ref, own=own):
            cj = slice(j * NB, j * NB + NB)
            o_ref[top:end, cj] = s_ref[top:end, cj] - times_transposed(
                o_ref[top:end, own], o_ref[cj, own]
            )

        update(kb + 1, lo, n)
        for j in range(kb + 2, steps):
            for top in range(j * NB, n, 2 * NB):
                waiting.append(functools.partial(update, j, top, min(n, top + 2 * NB)))


def factor_kernel(a_ref, o_ref):
    factor(a_ref, o_ref, lambda kb: None)


def factored(block):
    vmem = pl.BlockSpec(memory_space=pltpu.VMEM)
    n = block.shape[0]
    return pl.pallas_call(
        factor_kernel,
        out_shape=jax.ShapeDtypeStruct(block.shape, jnp.float32),
        in_specs=[vmem],
        out_specs=vmem,
        cost_estimate=pl.CostEstimate(flops=40 * n**3, bytes_accessed=8 * n * n, transcendentals=0),
        name="factor",
    )(block)


def solve_kernel(g_ref, f_ref, o_ref):
    n = f_ref.shape[0]
    o_ref[...] = g_ref[...]
    for kb in range(n // NB):
        own = slice(kb * NB, kb * NB + NB)
        x = times_transposed(o_ref[:, own], f_ref[own, own])
        o_ref[:, own] = x
        lo = (kb + 1) * NB
        if lo < n:
            o_ref[:, lo:] = o_ref[:, lo:] - times_transposed(x, f_ref[lo:, own])


def solved(rows, factor):
    vmem = pl.BlockSpec(memory_space=pltpu.VMEM)
    return pl.pallas_call(
        solve_kernel,
        out_shape=jax.ShapeDtypeStruct(rows.shape, jnp.float32),
        in_specs=[vmem, vmem],
        out_specs=vmem,
        name="solve",
    )(rows, factor)


MESH_IDS = pl.DeviceIdType.MESH
Z, X, Y, GROUPS = 8, 4, 4, 8
CHUNKS = 8
SAMPLES = 8192
AHEAD = 62


def here():
    samp, z, x = lax.axis_index("samp"), lax.axis_index("z"), lax.axis_index("x")
    return samp, z, x


def wrapped(value, size):
    return lax.rem(value + size, size)


def meet(peers):
    barrier = pltpu.get_barrier_semaphore()
    for peer in peers:
        pl.semaphore_signal(barrier, inc=1, device_id=peer, device_id_type=MESH_IDS)
    pl.semaphore_wait(barrier, len(peers))


def at(samp, z, x):
    return {"samp": samp, "z": z, "x": x}


def plane_peers(samp, z, x):
    return [
        (ds, dx, at(wrapped(samp + ds, GROUPS), z, wrapped(x + dx, X)))
        for ds in range(GROUPS)
        for dx in range(X)
        if (ds, dx) != (0, 0)
    ]


def column_peers(samp, z, x):
    return [(dz, at(samp, wrapped(z + dz, Z), x)) for dz in range(1, Z)]


def copy_to(src, dst, send, recv, peer):
    return pltpu.make_async_remote_copy(
        src_ref=src, dst_ref=dst, send_sem=send, recv_sem=recv,
        device_id=peer, device_id_type=MESH_IDS,
    )


def exchange_kernel(jac_ref, slot_ref, group_ref, tile_ref, pivot_ref, slots_ref,
                    own_sem, send, recv, zsend, zrecv, ps, pr, zs, zr):
    samp, z, x = here()
    right, left = wrapped(z + 1, Z), wrapped(z - 1, Z)
    column, plane = column_peers(samp, z, x), plane_peers(samp, z, x)
    me = at(samp, z, x)
    meet([peer for _, peer in column] + [peer for _, _, peer in plane])
    rows = jac_ref.shape[0]
    tile = tile_ref.shape[-1]
    wide = tile // CHUNKS
    sends = []

    def start(copy):
        copy.start()
        sends.append(copy)

    def arrived(ref, send_sem, recv_sem):
        copy_to(ref, ref, send_sem, recv_sem, me).wait_recv()

    def cols(q):
        return pl.ds(q * wide, wide)

    slots_ref[samp, z, x] = slot_ref[...]
    for ds, dx, peer in plane:
        start(copy_to(slot_ref, slots_ref.at[samp, z, x], ps.at[ds, dx], pr.at[ds, dx], peer))

    owns = []
    for q in range(CHUNKS):
        first = pl.multiple_of((samp * X + x) * tile + q * wide, wide)
        owns.append(pltpu.make_async_copy(jac_ref.at[:, pl.ds(first, wide)],
                                          tile_ref.at[samp, x, :, cols(q)], own_sem.at[q]))
        owns[-1].start()

    mixed = [plane[(7 * i) % len(plane)] for i in range(len(plane))]
    queue = [(q,) + target for q in range(CHUNKS) for target in mixed]

    def issue(count):
        for q, ds, dx, peer in queue[:count]:
            s, u = wrapped(samp + ds, GROUPS), wrapped(x + dx, X)
            first = pl.multiple_of((s * X + u) * tile + q * wide, wide)
            start(copy_to(jac_ref.at[:, pl.ds(first, wide)], tile_ref.at[samp, x, :, cols(q)],
                          send.at[q, ds, dx], recv.at[q, ds, dx], peer))
        del queue[:count]

    issue(AHEAD)
    for ds, dx, _ in plane:
        arrived(slots_ref.at[wrapped(samp - ds, GROUPS), z, wrapped(x - dx, X)],
                ps.at[ds, dx], pr.at[ds, dx])
    for dz, peer in column:
        ref = slots_ref.at[:, z]
        start(copy_to(ref, ref, zs.at[dz], zr.at[dz], peer))

    def hop(d, s, q):
        owner = wrapped(z - s, Z) if d == 0 else wrapped(z + s, Z)
        ref = pivot_ref.at[owner, :, :, cols(q)]
        start(copy_to(ref, ref, zsend.at[d, s, q], zrecv.at[d, s, q],
                      at(samp, right if d == 0 else left, x)))

    def came(d, s, q):
        owner = wrapped(z - 1 - s, Z) if d == 0 else wrapped(z + 1 + s, Z)
        arrived(pivot_ref.at[owner, :, :, cols(q)], zsend.at[d, s, q], zrecv.at[d, s, q])

    def farthest(d, q):
        return d == q % 2

    def forward(q, s):
        for d in range(2):
            came(d, s - 1, q)
            if s < 3 or farthest(d, q):
                hop(d, s, q)

    for tick in range(CHUNKS + 3):
        if tick < CHUNKS:
            q = tick
            for ds, dx, _ in plane:
                arrived(tile_ref.at[wrapped(samp - ds, GROUPS), wrapped(x - dx, X), :, cols(q)],
                        send.at[q, ds, dx], recv.at[q, ds, dx])
            owns[q].wait()
            picked = tile_ref[0, :, :, cols(q)]
            for g in range(1, GROUPS):
                picked = jnp.where(group_ref[0] == g, tile_ref[g, :, :, cols(q)], picked)
            pivot_ref[z, :, :, cols(q)] = picked
            for d in range(2):
                hop(d, 0, q)
            issue(8)
        for s in range(1, 4):
            if 0 <= tick - s < CHUNKS:
                forward(tick - s, s)
            issue(8)
    for q in range(CHUNKS):
        came(0 if farthest(0, q) else 1, 3, q)
    for dz, _ in column:
        arrived(slots_ref.at[:, wrapped(z - dz, Z)], zs.at[dz], zr.at[dz])
    for copy in sends:
        copy.wait_send()


def exchanged(jacobian, slots, group):
    vmem = pl.BlockSpec(memory_space=pltpu.VMEM)
    dma = pltpu.SemaphoreType.DMA
    rows, params = jacobian.shape
    tile = params // (GROUPS * X)
    return pl.pallas_call(
        exchange_kernel,
        out_shape=(
            jax.ShapeDtypeStruct((GROUPS, X, rows, tile), jacobian.dtype),
            jax.ShapeDtypeStruct((Z, X, rows, tile), jacobian.dtype),
            jax.ShapeDtypeStruct((GROUPS, Z, X, 1, 128), slots.dtype),
        ),
        in_specs=[pl.BlockSpec(memory_space=pl.ANY), vmem,
                  pl.BlockSpec(memory_space=pltpu.SMEM)],
        out_specs=(vmem, vmem, vmem),
        scratch_shapes=[dma((CHUNKS,)), dma((CHUNKS, GROUPS, X)), dma((CHUNKS, GROUPS, X)),
                        dma((2, 4, CHUNKS)), dma((2, 4, CHUNKS)),
                        dma((GROUPS, X)), dma((GROUPS, X)), dma((Z,)), dma((Z,))],
        compiler_params=pltpu.CompilerParams(collective_id=0, has_side_effects=True),
        name="exchange",
    )(jacobian, slots, group)


def rows_kernel(c_ref, o_ref, sib, acc, first0, first1, acc0, acc1, second0, second1,
                ss, sr, s0, r0, s1, r1, t0, q0, t1, q1):
    samp, z, x = here()
    y, core = samp // 2, lax.rem(samp, 2)
    sibling = at(2 * y + 1 - core, z, x)
    ring_y = [(d, wrapped(y + d, Y)) for d in range(1, Y)]
    ring_x = [(d, wrapped(x + d, X)) for d in range(1, X)]
    to_y = [at(2 * v + core, z, x) for _, v in ring_y]
    to_x = [at(samp, z, v) for _, v in ring_x]
    meet([sibling] + to_y + to_x)
    wide = c_ref.shape[4] // 2
    low, high = pl.ds(0, wide), pl.ds(wide, wide)
    sends = []

    def start(copy):
        copy.start()
        sends.append(copy)

    order = (2, 1, 3, 0)
    for d in order:
        v = wrapped(y + d, Y)
        start(copy_to(c_ref.at[v, 1 - core], sib.at[v], ss.at[d], sr.at[d], sibling))
    for d in order:
        v = wrapped(y + d, Y)
        copy_to(sib.at[v], sib.at[v], ss.at[d], sr.at[d], sibling).wait_recv()
        acc[v] = c_ref[v, core] + sib[v]
        if d:
            start(copy_to(acc.at[v, :, :, low], first0.at[d], s0.at[d], r0.at[d],
                          at(2 * v + core, z, x)))
    for d in (2, 1, 3):
        u = wrapped(x + d, X)
        start(copy_to(acc.at[:, u, :, high], first1.at[d], s1.at[d], r1.at[d], at(samp, z, u)))
    me = at(samp, z, x)
    for d in (1, 2, 3):
        copy_to(first0.at[d], first0.at[d], s0.at[d], r0.at[d], me).wait_recv()
    acc0[...] = acc[y, :, :, low] + first0[1] + first0[2] + first0[3]
    for d in (2, 1, 3):
        u = wrapped(x + d, X)
        start(copy_to(acc0.at[u], second0.at[d], t0.at[d], q0.at[d], at(samp, z, u)))
    for d in (1, 2, 3):
        copy_to(first1.at[d], first1.at[d], s1.at[d], r1.at[d], me).wait_recv()
    acc1[...] = acc[:, x, :, high] + first1[1] + first1[2] + first1[3]
    for d in (2, 1, 3):
        v = wrapped(y + d, Y)
        start(copy_to(acc1.at[v], second1.at[d], t1.at[d], q1.at[d], at(2 * v + core, z, x)))
    for d in (1, 2, 3):
        copy_to(second0.at[d], second0.at[d], t0.at[d], q0.at[d], me).wait_recv()
    o_ref[:, low] = acc0[x] + second0[1] + second0[2] + second0[3]
    for d in (1, 2, 3):
        copy_to(second1.at[d], second1.at[d], t1.at[d], q1.at[d], me).wait_recv()
    o_ref[:, high] = acc1[y] + second1[1] + second1[2] + second1[3]
    for copy in sends:
        copy.wait_send()


def summed_rows(partial):
    vmem = pl.BlockSpec(memory_space=pltpu.VMEM)
    dma = pltpu.SemaphoreType.DMA
    n = partial.shape[1]
    rows = partial.shape[0] // (GROUPS * X)
    wide = n // 2
    f32 = jnp.float32
    return pl.pallas_call(
        rows_kernel,
        out_shape=jax.ShapeDtypeStruct((rows, n), f32),
        in_specs=[vmem],
        out_specs=vmem,
        scratch_shapes=[
            pltpu.VMEM((Y, X, rows, n), f32), pltpu.VMEM((Y, X, rows, n), f32),
            pltpu.VMEM((Y, X, rows, wide), f32), pltpu.VMEM((X, Y, rows, wide), f32),
            pltpu.VMEM((X, rows, wide), f32), pltpu.VMEM((Y, rows, wide), f32),
            pltpu.VMEM((X, rows, wide), f32), pltpu.VMEM((Y, rows, wide), f32),
        ] + [dma((4,))] * 10,
        compiler_params=pltpu.CompilerParams(collective_id=1, has_side_effects=True),
        name="sum_rows",
    )(partial.reshape(Y, 2, X, rows, n))


def block_kernel(p_ref, shift_ref, o_ref, got, piece, ps, pr, zs, zr, xs, xr, ys, yr, ys2, yr2, xs2, xr2, cs, cr):
    samp, z, x = here()
    y, core = samp // 2, lax.rem(samp, 2)
    xh, xl = x // 2, lax.rem(x, 2)
    sibling = at(2 * y + 1 - core, z, x)
    column, plane = column_peers(samp, z, x), plane_peers(samp, z, x)
    meet([peer for _, peer in column] + [peer for _, _, peer in plane])
    me = at(samp, z, x)
    wide = p_ref.shape[4] // 2
    sends = []

    def start(copy):
        copy.start()
        sends.append(copy)

    def cols(xlow, color=None):
        if color is None:
            return pl.ds(pl.multiple_of(xlow * wide, wide), wide)
        return pl.ds(pl.multiple_of(xlow * wide + color * (wide // 2), wide // 2), wide // 2)

    def arrived(ref, send, recv):
        copy_to(ref, ref, send, recv, me).wait_recv()

    for ds, dx, peer in plane:
        s, u = wrapped(samp + ds, GROUPS), wrapped(x + dx, X)
        start(copy_to(p_ref.at[s // 2, lax.rem(s, 2), u // 2, :, cols(lax.rem(u, 2))],
                      got.at[ds, dx], ps.at[ds, dx], pr.at[ds, dx], peer))
    total = p_ref[y, core, xh, :, cols(xl)]
    for ds, dx, _ in plane:
        arrived(got.at[ds, dx], ps.at[ds, dx], pr.at[ds, dx])
    for ds, dx, _ in plane:
        total = total + got[ds, dx]
    shape = total.shape
    row = lax.broadcasted_iota(jnp.int32, shape, 0) + (z * 128 + (2 * samp + xh) * 8)
    column_id = lax.broadcasted_iota(jnp.int32, shape, 1) + xl * wide
    total = total / SAMPLES + jnp.where(row == column_id, shift_ref[0], 0.0)
    piece[...] = total
    o_ref[z, y, core, xh, :, cols(xl)] = total
    for dz, peer in column:
        start(copy_to(piece, o_ref.at[z, y, core, xh, :, cols(xl)], zs.at[dz], zr.at[dz], peer))
    for dz, _ in column:
        arrived(o_ref.at[wrapped(z - dz, Z), y, core, xh, :, cols(xl)], zs.at[dz], zr.at[dz])
    for d in (2, 1, 3):
        v, u = wrapped(y + d, Y), wrapped(x + d, X)
        ref0 = o_ref.at[:, y, core, xh, :, cols(xl, 0)]
        start(copy_to(ref0, ref0, xs.at[d], xr.at[d], at(samp, z, u)))
        ref1 = o_ref.at[:, y, core, xh, :, cols(xl, 1)]
        start(copy_to(ref1, ref1, ys.at[d], yr.at[d], at(2 * v + core, z, x)))
    for d in (1, 2, 3):
        u = wrapped(x - d, X)
        arrived(o_ref.at[:, y, core, u // 2, :, cols(lax.rem(u, 2), 0)], xs.at[d], xr.at[d])
    for d in (2, 1, 3):
        v = wrapped(y + d, Y)
        for low in range(2):
            ref = o_ref.at[:, y, core, :, :, cols(low, 0)]
            start(copy_to(ref, ref, ys2.at[d, low], yr2.at[d, low], at(2 * v + core, z, x)))
    for d in (1, 2, 3):
        v = wrapped(y - d, Y)
        arrived(o_ref.at[:, v, core, xh, :, cols(xl, 1)], ys.at[d], yr.at[d])
    for d in (2, 1, 3):
        u = wrapped(x + d, X)
        ref = o_ref.at[:, :, core, xh, :, cols(xl, 1)]
        start(copy_to(ref, ref, xs2.at[d], xr2.at[d], at(samp, z, u)))
    for d in (1, 3, 2):
        u = wrapped(x - d, X)
        arrived(o_ref.at[:, :, core, u // 2, :, cols(lax.rem(u, 2), 1)], xs2.at[d], xr2.at[d])
    for d in (0, 1, 3, 2):
        v = wrapped(y - d, Y)
        if d:
            for low in range(2):
                arrived(o_ref.at[:, v, core, :, :, cols(low, 0)], ys2.at[d, low], yr2.at[d, low])
        ref = o_ref.at[:, v, core]
        start(copy_to(ref, ref, cs.at[d], cr.at[d], sibling))
    for d in range(Y):
        arrived(o_ref.at[:, wrapped(y - d, Y), 1 - core], cs.at[d], cr.at[d])
    for copy in sends:
        copy.wait_send()


def summed_block(part, shift):
    vmem = pl.BlockSpec(memory_space=pltpu.VMEM)
    dma = pltpu.SemaphoreType.DMA
    band, n = part.shape
    f32 = jnp.float32
    out = pl.pallas_call(
        block_kernel,
        out_shape=jax.ShapeDtypeStruct((Z, Y, 2, 2, 8, n), f32),
        in_specs=[vmem, pl.BlockSpec(memory_space=pltpu.SMEM)],
        out_specs=vmem,
        scratch_shapes=[
            pltpu.VMEM((GROUPS, X, 8, n // 2), f32), pltpu.VMEM((8, n // 2), f32),
            dma((GROUPS, X)), dma((GROUPS, X)), dma((Z,)), dma((Z,)),
            dma((4,)), dma((4,)), dma((4,)), dma((4,)),
            dma((4, 2)), dma((4, 2)), dma((4,)), dma((4,)), dma((4,)), dma((4,)),
        ],
        compiler_params=pltpu.CompilerParams(collective_id=2, has_side_effects=True),
        name="sum_block",
    )(part.reshape(Y, 2, 2, 8, n), shift)
    return out.reshape(Z * band, n)


def on_device(jacobian, sample_slot, panel_index, shift_value):
    width = sample_slot.shape[0]
    group_width = width * lax.axis_size(PAR)
    samples = group_width * lax.axis_size("samp")
    pivot_group = panel_index[0] // group_width
    rotation = panel_index[0] % group_width
    band = group_width // lax.axis_size("z")
    padded = jnp.pad(sample_slot, (0, 128 - width)).reshape(1, 128)
    tile, raw, slots = exchanged(jacobian, padded, pivot_group.reshape(1))
    tile = tile.reshape(group_width, -1)
    raw = raw.reshape(group_width, -1)
    slots = slots[..., 0, :width].reshape(-1, group_width)
    own_slots = lax.dynamic_index_in_dim(slots, lax.axis_index("samp"), 0, keepdims=False)
    pivot_slots = lax.dynamic_index_in_dim(slots, pivot_group, 0, keepdims=False)
    column = jnp.arange(group_width, dtype=jnp.int32)
    chosen = (pivot_slots[None, :] == ((column + rotation) % group_width)[:, None]).astype(jnp.bfloat16)

    pivot = lax.dot_general(
        chosen, raw, (((1,), (0,)), ((), ())), preferred_element_type=jnp.float32
    ).astype(jnp.bfloat16)

    contract = (((1,), (1,)), ((), ()))
    part = lax.dynamic_slice_in_dim(pivot, lax.axis_index("z") * band, band, 0)
    pivot_part = lax.dot_general(part, pivot, contract, preferred_element_type=jnp.float32)
    partial = lax.dot_general(tile, pivot, contract, preferred_element_type=jnp.float32)
    rows = summed_rows(partial)
    group_rows = lax.all_gather(rows, PAR, axis=0, tiled=True)
    block = summed_block(pivot_part, shift_value)
    position = lax.axis_index(PAR) * width + jnp.arange(width, dtype=jnp.int32)
    hit = own_slots[None, :] == position[:, None]
    source = jnp.sum(jnp.where(hit, column[None, :], 0), axis=1)
    my_rows = jnp.take(group_rows, source, axis=0) / samples
    on_pivot = lax.axis_index("samp") == pivot_group
    shifted = position[:, None] == ((column + rotation) % group_width)[None, :]
    my_rows = my_rows + jnp.where(shifted & on_pivot, shift_value[0], 0.0)
    return solved(my_rows, factored(block))


def solution(mesh):
    torus = Mesh(mesh.devices.reshape(mesh.shape["samp"], 8, 4), ("samp", "z", "x"))
    return jax.shard_map(
        on_device,
        mesh=torus,
        in_specs=(P(ALL, None), P(ALL), P(), P()),
        out_specs=P(ALL, None),
        check_vma=False,
    )
```

```python
import functools

import jax
import jax.numpy as jnp
from jax import lax
from jax.experimental import pallas as pl
from jax.experimental.pallas import tpu as pltpu
from jax.sharding import Mesh
from jax.sharding import PartitionSpec as P

PAR = ("z", "x")
PLANE = ("samp", "x")
ALL = ("samp", "z", "x")
NB = 128
STEP = 16
HI = lax.Precision.HIGHEST


def rank_update(r):
    h = r.astype(jnp.bfloat16).astype(jnp.float32)
    m = (r - h).astype(jnp.bfloat16).astype(jnp.float32)
    l = (r - h - m).astype(jnp.bfloat16).astype(jnp.float32)
    lhs = jnp.concatenate([h, h, m, h, l, m], 0).astype(jnp.bfloat16)
    rhs = jnp.concatenate([h, m, h, l, h, m], 0).astype(jnp.bfloat16)
    return lax.dot_general(
        lhs, rhs, (((0,), (0,)), ((), ())), preferred_element_type=jnp.float32
    )


def inverse_of_factor(block, filler):
    n = block.shape[0]
    groups = n // STEP
    rows = [block[STEP * i : STEP * i + STEP, :] for i in range(groups)]
    sub = lax.broadcasted_iota(jnp.int32, (STEP, n), 0)
    lane = lax.broadcasted_iota(jnp.int32, (STEP, n), 1)
    for b in range(groups):
        first = STEP * b
        r = rows[b]
        cols = [jnp.broadcast_to(r[:, first + j : first + j + 1], (STEP, n)) for j in range(STEP)]
        inside = (lane >= first) & (lane < first + STEP)
        r = jnp.where(inside, jnp.where(lane == sub + first, 1.0, 0.0), r)
        diag = jnp.ones((STEP, n), jnp.float32)
        for j in range(STEP):
            d = jnp.broadcast_to(cols[j][j : j + 1, :], (8, n))
            diag = jnp.where(sub == j, jnp.concatenate([d] * (STEP // 8), 0), diag)
            if j == STEP - 1:
                break
            low = (j + 1) // 8 * 8
            below = (STEP - low) // 8
            q = pl.reciprocal(d, approx=True)
            e = jnp.concatenate([1.0 - d * q] * below, 0)
            m = jnp.where(sub[low:] > j, cols[j][low:], 0.0) * jnp.concatenate([q] * below, 0)
            m = m + m * e

            def eliminated(v):
                left = v[low:] - m * jnp.broadcast_to(v[j : j + 1, :], (STEP - low, n))
                return left if low == 0 else jnp.concatenate([v[:low], left], 0)

            for c in range(j + 1, STEP):
                cols[c] = eliminated(cols[c])
            r = eliminated(r)
        s = lax.rsqrt(diag)
        s = s * (1.5 - 0.5 * diag * s * s)
        r = r * s
        rows[b] = r
        if b < groups - 1:
            p = rank_update(r)
            for i in range(b + 1, groups):
                rows[i] = jnp.where(inside, 0.0, rows[i]) - p[STEP * i : STEP * i + STEP, :]
        filler()
    kept = [jnp.where(lane <= sub + STEP * b, rows[b], 0.0) for b in range(groups)]
    return jnp.concatenate(kept, 0)


def times_transposed(a, b):
    return lax.dot_general(
        a, b, (((1,), (1,)), ((), ())), precision=HI, preferred_element_type=jnp.float32
    )


def factor_kernel(a_ref, g_ref, x_ref, o_ref):
    n = a_ref.shape[0]
    steps = n // NB
    waiting = []

    def run(count):
        for _ in range(min(count, len(waiting))):
            waiting.pop(0)()

    x_ref[...] = g_ref[...]
    for kb in range(steps):
        s_ref = a_ref if kb == 0 else o_ref
        own = slice(kb * NB, kb * NB + NB)
        share = -(-len(waiting) // (NB // STEP))
        w = inverse_of_factor(s_ref[own, own], lambda: run(share))
        run(len(waiting))
        lo = (kb + 1) * NB
        x_ref[:, own] = times_transposed(x_ref[:, own], w)
        if kb == steps - 1:
            break
        o_ref[lo:, own] = times_transposed(s_ref[lo:, own], w)

        def update(j, top, end, s_ref=s_ref, own=own):
            cj = slice(j * NB, j * NB + NB)
            o_ref[top:end, cj] = s_ref[top:end, cj] - times_transposed(
                o_ref[top:end, own], o_ref[cj, own]
            )

        def advance(left, end, own=own):
            x_ref[:, left:end] = x_ref[:, left:end] - times_transposed(
                x_ref[:, own], o_ref[left:end, own]
            )

        update(kb + 1, lo, n)
        waiting.append(functools.partial(advance, lo, n))
        for j in range(kb + 2, steps):
            for top in range(j * NB, n, 2 * NB):
                waiting.append(functools.partial(update, j, top, min(n, top + 2 * NB)))


def solved(rows, block):
    vmem = pl.BlockSpec(memory_space=pltpu.VMEM)
    return pl.pallas_call(
        factor_kernel,
        out_shape=jax.ShapeDtypeStruct(rows.shape, jnp.float32),
        in_specs=[vmem, vmem],
        out_specs=vmem,
        scratch_shapes=[pltpu.VMEM(block.shape, jnp.float32)],
        name="factor",
    )(block, rows)


MESH_IDS = pl.DeviceIdType.MESH
Z, X, Y, GROUPS = 8, 4, 4, 8
CHUNKS = 8
SAMPLES = 8192
AHEAD = 62


def here():
    samp, z, x = lax.axis_index("samp"), lax.axis_index("z"), lax.axis_index("x")
    return samp, z, x


def wrapped(value, size):
    return lax.rem(value + size, size)


def meet(peers):
    barrier = pltpu.get_barrier_semaphore()
    for peer in peers:
        pl.semaphore_signal(barrier, inc=1, device_id=peer, device_id_type=MESH_IDS)
    pl.semaphore_wait(barrier, len(peers))


def at(samp, z, x):
    return {"samp": samp, "z": z, "x": x}


def plane_peers(samp, z, x):
    return [
        (ds, dx, at(wrapped(samp + ds, GROUPS), z, wrapped(x + dx, X)))
        for ds in range(GROUPS)
        for dx in range(X)
        if (ds, dx) != (0, 0)
    ]


def column_peers(samp, z, x):
    return [(dz, at(samp, wrapped(z + dz, Z), x)) for dz in range(1, Z)]


def copy_to(src, dst, send, recv, peer):
    return pltpu.make_async_remote_copy(
        src_ref=src, dst_ref=dst, send_sem=send, recv_sem=recv,
        device_id=peer, device_id_type=MESH_IDS,
    )


def exchange_kernel(jac_ref, slot_ref, group_ref, tile_ref, pivot_ref, slots_ref,
                    near, own_sem, send, recv, zsend, zrecv, ps, pr, zs, zr):
    samp, z, x = here()
    right, left = wrapped(z + 1, Z), wrapped(z - 1, Z)
    column, plane = column_peers(samp, z, x), plane_peers(samp, z, x)
    me = at(samp, z, x)
    meet([peer for _, peer in column] + [peer for _, _, peer in plane])
    rows = jac_ref.shape[0]
    tile = tile_ref.shape[-1]
    wide = tile // CHUNKS
    sends = []

    def start(copy):
        copy.start()
        sends.append(copy)

    def arrived(ref, send_sem, recv_sem):
        copy_to(ref, ref, send_sem, recv_sem, me).wait_recv()

    def cols(q):
        return pl.ds(q * wide, wide)

    near[samp, x] = slot_ref[...]
    for ds, dx, peer in plane:
        start(copy_to(slot_ref, near.at[samp, x], ps.at[ds, dx], pr.at[ds, dx], peer))

    owns = []
    for q in range(CHUNKS):
        first = pl.multiple_of((samp * X + x) * tile + q * wide, wide)
        owns.append(pltpu.make_async_copy(jac_ref.at[:, pl.ds(first, wide)],
                                          tile_ref.at[samp, x, :, cols(q)], own_sem.at[q]))
        owns[-1].start()

    mixed = [plane[(7 * i) % len(plane)] for i in range(len(plane))]
    queue = [(q,) + target for q in range(CHUNKS) for target in mixed]

    def issue(count):
        for q, ds, dx, peer in queue[:count]:
            s, u = wrapped(samp + ds, GROUPS), wrapped(x + dx, X)
            first = pl.multiple_of((s * X + u) * tile + q * wide, wide)
            start(copy_to(jac_ref.at[:, pl.ds(first, wide)], tile_ref.at[samp, x, :, cols(q)],
                          send.at[q, ds, dx], recv.at[q, ds, dx], peer))
        del queue[:count]

    issue(AHEAD)
    for ds, dx, _ in plane:
        arrived(near.at[wrapped(samp - ds, GROUPS), wrapped(x - dx, X)],
                ps.at[ds, dx], pr.at[ds, dx])
    row = lax.broadcasted_iota(jnp.int32, (GROUPS, 128), 0)
    joined = jnp.zeros((GROUPS, 128), jnp.int32)
    for g in range(GROUPS):
        line = near[g, 0] + near[g, 1] + near[g, 2] + near[g, 3]
        joined = jnp.where(row == g, line, joined)
    slots_ref[z] = joined
    for dz, peer in column:
        ref = slots_ref.at[z]
        start(copy_to(ref, ref, zs.at[dz], zr.at[dz], peer))

    def hop(d, s, q):
        owner = wrapped(z - s, Z) if d == 0 else wrapped(z + s, Z)
        ref = pivot_ref.at[owner, :, :, cols(q)]
        start(copy_to(ref, ref, zsend.at[d, s, q], zrecv.at[d, s, q],
                      at(samp, right if d == 0 else left, x)))

    def came(d, s, q):
        owner = wrapped(z - 1 - s, Z) if d == 0 else wrapped(z + 1 + s, Z)
        arrived(pivot_ref.at[owner, :, :, cols(q)], zsend.at[d, s, q], zrecv.at[d, s, q])

    def farthest(d, q):
        return d == q % 2

    def forward(q, s):
        for d in range(2):
            came(d, s - 1, q)
            if s < 3 or farthest(d, q):
                hop(d, s, q)

    for tick in range(CHUNKS + 3):
        if tick < CHUNKS:
            q = tick
            for ds, dx, _ in plane:
                arrived(tile_ref.at[wrapped(samp - ds, GROUPS), wrapped(x - dx, X), :, cols(q)],
                        send.at[q, ds, dx], recv.at[q, ds, dx])
            owns[q].wait()
            picked = tile_ref[0, :, :, cols(q)]
            for g in range(1, GROUPS):
                picked = jnp.where(group_ref[0] == g, tile_ref[g, :, :, cols(q)], picked)
            pivot_ref[z, :, :, cols(q)] = picked
            for d in range(2):
                hop(d, 0, q)
            issue(8)
        for s in range(1, 4):
            if 0 <= tick - s < CHUNKS:
                forward(tick - s, s)
            issue(8)
    for q in range(CHUNKS):
        came(0 if farthest(0, q) else 1, 3, q)
    for dz, _ in column:
        arrived(slots_ref.at[wrapped(z - dz, Z)], zs.at[dz], zr.at[dz])
    for copy in sends:
        copy.wait_send()


def exchanged(jacobian, slots, group):
    vmem = pl.BlockSpec(memory_space=pltpu.VMEM)
    dma = pltpu.SemaphoreType.DMA
    rows, params = jacobian.shape
    tile = params // (GROUPS * X)
    return pl.pallas_call(
        exchange_kernel,
        out_shape=(
            jax.ShapeDtypeStruct((GROUPS, X, rows, tile), jacobian.dtype),
            jax.ShapeDtypeStruct((Z, X, rows, tile), jacobian.dtype),
            jax.ShapeDtypeStruct((Z, GROUPS, 128), slots.dtype),
        ),
        in_specs=[pl.BlockSpec(memory_space=pl.ANY), vmem,
                  pl.BlockSpec(memory_space=pltpu.SMEM)],
        out_specs=(vmem, vmem, vmem),
        scratch_shapes=[pltpu.VMEM((GROUPS, X, 1, 128), slots.dtype),
                        dma((CHUNKS,)), dma((CHUNKS, GROUPS, X)), dma((CHUNKS, GROUPS, X)),
                        dma((2, 4, CHUNKS)), dma((2, 4, CHUNKS)),
                        dma((GROUPS, X)), dma((GROUPS, X)), dma((Z,)), dma((Z,))],
        compiler_params=pltpu.CompilerParams(collective_id=0, has_side_effects=True),
        name="exchange",
    )(jacobian, slots, group)


def reduce_kernel(p_ref, c_ref, pick_ref, place_ref, shift_ref, o_ref, g_ref,
                  got, piece, sib, acc, first0, first1, acc0, acc1, second0, second1,
                  part, column_rows, chosen, third,
                  ps, pr, zs, zr, xs, xr, ys, yr, ys2, yr2, xs2, xr2, cs, cr,
                  ss, sr, s0, r0, s1, r1, t0, q0, t1, q1, us, ur, vs, vr):
    samp, z, x = here()
    y, core = samp // 2, lax.rem(samp, 2)
    xh, xl = x // 2, lax.rem(x, 2)
    me, sibling = at(samp, z, x), at(2 * y + 1 - core, z, x)
    column, plane = column_peers(samp, z, x), plane_peers(samp, z, x)
    meet([peer for _, peer in column] + [peer for _, _, peer in plane])
    n = p_ref.shape[4]
    wide = n // 2
    low, high = pl.ds(0, wide), pl.ds(wide, wide)
    order = (2, 1, 3)
    sends = []

    def start(copy):
        copy.start()
        sends.append(copy)

    def arrived(ref, send, recv):
        copy_to(ref, ref, send, recv, me).wait_recv()

    def cols(xlow, color=None):
        if color is None:
            return pl.ds(pl.multiple_of(xlow * wide, wide), wide)
        return pl.ds(pl.multiple_of(xlow * wide + color * (wide // 2), wide // 2), wide // 2)

    def up(d):
        v = wrapped(y + d, Y)
        return v, at(2 * v + core, z, x)

    def along(d):
        u = wrapped(x + d, X)
        return u, at(samp, z, u)

    for ds, dx, peer in plane:
        s, u = wrapped(samp + ds, GROUPS), wrapped(x + dx, X)
        start(copy_to(p_ref.at[s // 2, lax.rem(s, 2), u // 2, :, cols(lax.rem(u, 2))],
                      got.at[ds, dx], ps.at[ds, dx], pr.at[ds, dx], peer))
    for d in order + (0,):
        v, _ = up(d)
        start(copy_to(c_ref.at[v, 1 - core], sib.at[v], ss.at[d], sr.at[d], sibling))
    for d in order + (0,):
        v, peer = up(d)
        arrived(sib.at[v], ss.at[d], sr.at[d])
        acc[v] = c_ref[v, core] + sib[v]
        if d:
            start(copy_to(acc.at[v, :, :, low], first0.at[d], s0.at[d], r0.at[d], peer))
    for d in order:
        u, peer = along(d)
        start(copy_to(acc.at[:, u, :, high], first1.at[d], s1.at[d], r1.at[d], peer))

    total = p_ref[y, core, xh, :, cols(xl)]
    for ds, dx, _ in plane:
        arrived(got.at[ds, dx], ps.at[ds, dx], pr.at[ds, dx])
    for ds, dx, _ in plane:
        total = total + got[ds, dx]
    shape = total.shape
    row = lax.broadcasted_iota(jnp.int32, shape, 0) + (z * 128 + (2 * samp + xh) * 8)
    column_id = lax.broadcasted_iota(jnp.int32, shape, 1) + xl * wide
    total = total / SAMPLES + jnp.where(row == column_id, shift_ref[0], 0.0)
    piece[...] = total
    o_ref[z, y, core, xh, :, cols(xl)] = total
    for dz, peer in column:
        start(copy_to(piece, o_ref.at[z, y, core, xh, :, cols(xl)], zs.at[dz], zr.at[dz], peer))
    for dz, _ in column:
        arrived(o_ref.at[wrapped(z - dz, Z), y, core, xh, :, cols(xl)], zs.at[dz], zr.at[dz])
    for d in order:
        ref0 = o_ref.at[:, y, core, xh, :, cols(xl, 0)]
        start(copy_to(ref0, ref0, xs.at[d], xr.at[d], along(d)[1]))
        ref1 = o_ref.at[:, y, core, xh, :, cols(xl, 1)]
        start(copy_to(ref1, ref1, ys.at[d], yr.at[d], up(d)[1]))

    for d in order:
        arrived(first0.at[d], s0.at[d], r0.at[d])
    acc0[...] = acc[y, :, :, low] + first0[1] + first0[2] + first0[3]
    for d in order:
        u, peer = along(d)
        start(copy_to(acc0.at[u], second0.at[d], t0.at[d], q0.at[d], peer))
    for d in order:
        arrived(first1.at[d], s1.at[d], r1.at[d])
    acc1[...] = acc[:, x, :, high] + first1[1] + first1[2] + first1[3]
    for d in order:
        v, peer = up(d)
        start(copy_to(acc1.at[v], second1.at[d], t1.at[d], q1.at[d], peer))

    for d in order:
        u = wrapped(x - d, X)
        arrived(o_ref.at[:, y, core, u // 2, :, cols(lax.rem(u, 2), 0)], xs.at[d], xr.at[d])
    for d in order:
        for half in range(2):
            ref = o_ref.at[:, y, core, :, :, cols(half, 0)]
            start(copy_to(ref, ref, ys2.at[d, half], yr2.at[d, half], up(d)[1]))
    for d in order:
        v = wrapped(y - d, Y)
        arrived(o_ref.at[:, v, core, xh, :, cols(xl, 1)], ys.at[d], yr.at[d])
    for d in order:
        ref = o_ref.at[:, :, core, xh, :, cols(xl, 1)]
        start(copy_to(ref, ref, xs2.at[d], xr2.at[d], along(d)[1]))

    for d in order:
        arrived(second0.at[d], t0.at[d], q0.at[d])
        arrived(second1.at[d], t1.at[d], q1.at[d])
    part[:, low] = acc0[x] + second0[1] + second0[2] + second0[3]
    part[:, high] = acc1[y] + second1[1] + second1[2] + second1[3]
    column_rows[z] = part[...]
    for dz, peer in column:
        start(copy_to(part, column_rows.at[z], us.at[dz], ur.at[dz], peer))

    for d in order:
        u = wrapped(x - d, X)
        arrived(o_ref.at[:, :, core, u // 2, :, cols(lax.rem(u, 2), 1)], xs2.at[d], xr2.at[d])
    for d in (0,) + order:
        v = wrapped(y - d, Y)
        if d:
            for half in range(2):
                arrived(o_ref.at[:, v, core, :, :, cols(half, 0)], ys2.at[d, half], yr2.at[d, half])
        ref = o_ref.at[:, v, core]
        start(copy_to(ref, ref, cs.at[d], cr.at[d], sibling))

    for dz, _ in column:
        arrived(column_rows.at[wrapped(z - dz, Z)], us.at[dz], ur.at[dz])
    rest = column_rows[...].reshape(pick_ref.shape[1], n)
    moved = jnp.zeros((pick_ref.shape[0], n), jnp.float32)
    for _ in range(3):
        head = rest.astype(jnp.bfloat16)
        rest = rest - head.astype(jnp.float32)
        moved = moved + lax.dot_general(
            pick_ref[...], head, (((1,), (0,)), ((), ())), preferred_element_type=jnp.float32
        )
    chosen[...] = moved.reshape(chosen.shape)
    for d in order:
        u, peer = along(d)
        start(copy_to(chosen.at[u], third.at[d], vs.at[d], vr.at[d], peer))
    width = chosen.shape[1]
    position = lax.broadcasted_iota(jnp.int32, (width, n), 0) + (z * X + x) * width
    column_id = lax.broadcasted_iota(jnp.int32, (width, n), 1)
    on_pivot = jnp.where(position == lax.rem(column_id + place_ref[1], n), shift_ref[0], 0.0)
    on_pivot = jnp.where(place_ref[0] == samp, on_pivot, 0.0)
    for d in order:
        arrived(third.at[d], vs.at[d], vr.at[d])
    g_ref[...] = (chosen[x] + third[1] + third[2] + third[3]) / SAMPLES + on_pivot
    for d in range(Y):
        arrived(o_ref.at[:, wrapped(y - d, Y), 1 - core], cs.at[d], cr.at[d])
    for copy in sends:
        copy.wait_send()


def reduced(part, partial, pick, place, shift):
    vmem = pl.BlockSpec(memory_space=pltpu.VMEM)
    smem = pl.BlockSpec(memory_space=pltpu.SMEM)
    dma = pltpu.SemaphoreType.DMA
    band, n = part.shape
    rows = partial.shape[0] // (GROUPS * X)
    wide = n // 2
    f32 = jnp.float32
    block, my_rows = pl.pallas_call(
        reduce_kernel,
        out_shape=(jax.ShapeDtypeStruct((Z, Y, 2, 2, 8, n), f32),
                   jax.ShapeDtypeStruct((rows, n), f32)),
        in_specs=[vmem, vmem, vmem, smem, smem],
        out_specs=(vmem, vmem),
        scratch_shapes=[
            pltpu.VMEM((GROUPS, X, 8, wide), f32), pltpu.VMEM((8, wide), f32),
            pltpu.VMEM((Y, X, rows, n), f32), pltpu.VMEM((Y, X, rows, n), f32),
            pltpu.VMEM((Y, X, rows, wide), f32), pltpu.VMEM((X, Y, rows, wide), f32),
            pltpu.VMEM((X, rows, wide), f32), pltpu.VMEM((Y, rows, wide), f32),
            pltpu.VMEM((X, rows, wide), f32), pltpu.VMEM((Y, rows, wide), f32),
            pltpu.VMEM((rows, n), f32), pltpu.VMEM((Z, rows, n), f32),
            pltpu.VMEM((X, rows, n), f32), pltpu.VMEM((X, rows, n), f32),
            dma((GROUPS, X)), dma((GROUPS, X)), dma((Z,)), dma((Z,)),
            dma((4,)), dma((4,)), dma((4,)), dma((4,)),
            dma((4, 2)), dma((4, 2)), dma((4,)), dma((4,)), dma((4,)), dma((4,)),
        ] + [dma((4,))] * 10 + [dma((Z,)), dma((Z,)), dma((4,)), dma((4,))],
        compiler_params=pltpu.CompilerParams(collective_id=1, has_side_effects=True),
        name="reduce",
    )(part.reshape(Y, 2, 2, 8, n), partial.reshape(Y, 2, X, rows, n), pick, place, shift)
    return block.reshape(Z * band, n), my_rows


def on_device(jacobian, sample_slot, panel_index, shift_value):
    width = sample_slot.shape[0]
    group_width = width * lax.axis_size(PAR)
    samples = group_width * lax.axis_size("samp")
    pivot_group = panel_index[0] // group_width
    rotation = panel_index[0] % group_width
    band = group_width // lax.axis_size("z")
    lanes = jnp.tile(sample_slot, X).reshape(1, width * X)
    own_lanes = jnp.arange(width * X, dtype=jnp.int32)[None, :] // width == lax.axis_index("x")
    padded = jnp.where(own_lanes, lanes, 0)
    tile, raw, slots = exchanged(jacobian, padded, pivot_group.reshape(1))
    tile = tile.reshape(group_width, -1)
    raw = raw.reshape(group_width, -1)
    own_slots = lax.dynamic_index_in_dim(slots, lax.axis_index("samp"), 1, keepdims=False)
    pivot_slots = lax.dynamic_index_in_dim(slots, pivot_group, 1, keepdims=False).reshape(-1)
    column = jnp.arange(group_width, dtype=jnp.int32)
    chosen = (pivot_slots[None, :] == ((column + rotation) % group_width)[:, None]).astype(jnp.bfloat16)

    pivot = lax.dot_general(
        chosen, raw, (((1,), (0,)), ((), ())), preferred_element_type=jnp.float32
    ).astype(jnp.bfloat16)

    contract = (((1,), (1,)), ((), ()))
    part = lax.dynamic_slice_in_dim(pivot, lax.axis_index("z") * band, band, 0)
    pivot_part = lax.dot_general(part, pivot, contract, preferred_element_type=jnp.float32)
    partial = lax.dot_general(tile, pivot, contract, preferred_element_type=jnp.float32)
    sources = own_slots.reshape(-1, X, width)
    sources = lax.dynamic_index_in_dim(sources, lax.axis_index("x"), 1, keepdims=False)
    target = lax.axis_index("z") * band + jnp.arange(band, dtype=jnp.int32)
    pick = (target[:, None] == sources.reshape(1, -1)).astype(jnp.bfloat16)
    place = jnp.stack([pivot_group, rotation])
    block, my_rows = reduced(pivot_part, partial, pick, place, shift_value)
    return solved(my_rows, block)


def solution(mesh):
    torus = Mesh(mesh.devices.reshape(mesh.shape["samp"], 8, 4), ("samp", "z", "x"))
    return jax.shard_map(
        on_device,
        mesh=torus,
        in_specs=(P(ALL, None), P(ALL), P(), P()),
        out_specs=P(ALL, None),
        check_vma=False,
    )
```

```python
import functools

import jax
import jax.numpy as jnp
from jax import lax
from jax.experimental import pallas as pl
from jax.experimental.pallas import tpu as pltpu
from jax.sharding import Mesh
from jax.sharding import PartitionSpec as P

PAR = ("z", "x")
PLANE = ("samp", "x")
ALL = ("samp", "z", "x")
NB = 128
STEP = 16
HI = lax.Precision.HIGHEST


def rank_update(r):
    h = r.astype(jnp.bfloat16).astype(jnp.float32)
    m = (r - h).astype(jnp.bfloat16).astype(jnp.float32)
    l = (r - h - m).astype(jnp.bfloat16).astype(jnp.float32)
    lhs = jnp.concatenate([h, h, m, h, l, m], 0).astype(jnp.bfloat16)
    rhs = jnp.concatenate([h, m, h, l, h, m], 0).astype(jnp.bfloat16)
    return lax.dot_general(
        lhs, rhs, (((0,), (0,)), ((), ())), preferred_element_type=jnp.float32
    )


def inverse_of_factor(block, filler):
    n = block.shape[0]
    groups = n // STEP
    rows = [block[STEP * i : STEP * i + STEP, :] for i in range(groups)]
    sub = lax.broadcasted_iota(jnp.int32, (STEP, n), 0)
    lane = lax.broadcasted_iota(jnp.int32, (STEP, n), 1)
    for b in range(groups):
        first = STEP * b
        r = rows[b]
        cols = [jnp.broadcast_to(r[:, first + j : first + j + 1], (STEP, n)) for j in range(STEP)]
        inside = (lane >= first) & (lane < first + STEP)
        r = jnp.where(inside, jnp.where(lane == sub + first, 1.0, 0.0), r)
        diag = jnp.ones((STEP, n), jnp.float32)
        for j in range(STEP):
            d = jnp.broadcast_to(cols[j][j : j + 1, :], (8, n))
            diag = jnp.where(sub == j, jnp.concatenate([d] * (STEP // 8), 0), diag)
            if j == STEP - 1:
                break
            low = (j + 1) // 8 * 8
            below = (STEP - low) // 8
            q = pl.reciprocal(d, approx=True)
            e = jnp.concatenate([1.0 - d * q] * below, 0)
            m = jnp.where(sub[low:] > j, cols[j][low:], 0.0) * jnp.concatenate([q] * below, 0)
            m = m + m * e

            def eliminated(v):
                left = v[low:] - m * jnp.broadcast_to(v[j : j + 1, :], (STEP - low, n))
                return left if low == 0 else jnp.concatenate([v[:low], left], 0)

            for c in range(j + 1, STEP):
                cols[c] = eliminated(cols[c])
            r = eliminated(r)
        s = lax.rsqrt(diag)
        s = s * (1.5 - 0.5 * diag * s * s)
        r = r * s
        rows[b] = r
        if b < groups - 1:
            p = rank_update(r)
            for i in range(b + 1, groups):
                rows[i] = jnp.where(inside, 0.0, rows[i]) - p[STEP * i : STEP * i + STEP, :]
        filler()
    kept = [jnp.where(lane <= sub + STEP * b, rows[b], 0.0) for b in range(groups)]
    return jnp.concatenate(kept, 0)


def times_transposed(a, b):
    return lax.dot_general(
        a, b, (((1,), (1,)), ((), ())), precision=HI, preferred_element_type=jnp.float32
    )


def factor_kernel(a_ref, g_ref, x_ref, o_ref):
    n = a_ref.shape[0]
    steps = n // NB
    waiting = []

    def run(count):
        for _ in range(min(count, len(waiting))):
            waiting.pop(0)()

    x_ref[...] = g_ref[...]
    for kb in range(steps):
        s_ref = a_ref if kb == 0 else o_ref
        own = slice(kb * NB, kb * NB + NB)
        share = -(-len(waiting) // (NB // STEP))
        w = inverse_of_factor(s_ref[own, own], lambda: run(share))
        run(len(waiting))
        lo = (kb + 1) * NB
        x_ref[:, own] = times_transposed(x_ref[:, own], w)
        if kb == steps - 1:
            break
        o_ref[lo:, own] = times_transposed(s_ref[lo:, own], w)

        def update(j, top, end, s_ref=s_ref, own=own):
            cj = slice(j * NB, j * NB + NB)
            o_ref[top:end, cj] = s_ref[top:end, cj] - times_transposed(
                o_ref[top:end, own], o_ref[cj, own]
            )

        def advance(left, end, own=own):
            x_ref[:, left:end] = x_ref[:, left:end] - times_transposed(
                x_ref[:, own], o_ref[left:end, own]
            )

        update(kb + 1, lo, n)
        waiting.append(functools.partial(advance, lo, n))
        for j in range(kb + 2, steps):
            for top in range(j * NB, n, 2 * NB):
                waiting.append(functools.partial(update, j, top, min(n, top + 2 * NB)))


def solved(rows, block):
    vmem = pl.BlockSpec(memory_space=pltpu.VMEM)
    return pl.pallas_call(
        factor_kernel,
        out_shape=jax.ShapeDtypeStruct(rows.shape, jnp.float32),
        in_specs=[vmem, vmem],
        out_specs=vmem,
        scratch_shapes=[pltpu.VMEM(block.shape, jnp.float32)],
        name="factor",
    )(block, rows)


MESH_IDS = pl.DeviceIdType.MESH
Z, X, Y, GROUPS = 8, 4, 4, 8
CHUNKS = 8
SAMPLES = 8192
LEAD = 2


def here():
    samp, z, x = lax.axis_index("samp"), lax.axis_index("z"), lax.axis_index("x")
    return samp, z, x


def wrapped(value, size):
    return lax.rem(value + size, size)


def meet(peers):
    barrier = pltpu.get_barrier_semaphore()
    for peer in peers:
        pl.semaphore_signal(barrier, inc=1, device_id=peer, device_id_type=MESH_IDS)
    pl.semaphore_wait(barrier, len(peers))


def at(samp, z, x):
    return {"samp": samp, "z": z, "x": x}


def plane_peers(samp, z, x):
    return [
        (ds, dx, at(wrapped(samp + ds, GROUPS), z, wrapped(x + dx, X)))
        for ds in range(GROUPS)
        for dx in range(X)
        if (ds, dx) != (0, 0)
    ]


def column_peers(samp, z, x):
    return [(dz, at(samp, wrapped(z + dz, Z), x)) for dz in range(1, Z)]


def copy_to(src, dst, send, recv, peer):
    return pltpu.make_async_remote_copy(
        src_ref=src, dst_ref=dst, send_sem=send, recv_sem=recv,
        device_id=peer, device_id_type=MESH_IDS,
    )


def exchange_kernel(jac_ref, slot_ref, place_ref, c_ref, p_ref, slots_ref,
                    tile_ref, pivot_ref, near, matched, ordered,
                    own_sem, send, recv, zsend, zrecv, ps, pr, zs, zr):
    samp, z, x = here()
    right, left = wrapped(z + 1, Z), wrapped(z - 1, Z)
    column, plane = column_peers(samp, z, x), plane_peers(samp, z, x)
    me = at(samp, z, x)
    meet([peer for _, peer in column] + [peer for _, _, peer in plane])
    wide = tile_ref.shape[-1]
    n = ordered.shape[0]
    others = GROUPS * X - 1
    sends = []

    def start(copy):
        copy.start()
        sends.append(copy)

    def arrived(ref, send_sem, recv_sem):
        copy_to(ref, ref, send_sem, recv_sem, me).wait_recv()

    def columns(s, u, q):
        first = pl.multiple_of(((s * X + u) * CHUNKS + q) * wide, wide)
        return jac_ref.at[:, pl.ds(first, wide)]

    def within(q, i):
        turn = lax.rem(7 * i, others) + 1
        ds, dx = turn // X, lax.rem(turn, X)
        s, u = wrapped(samp + ds, GROUPS), wrapped(x + dx, X)
        return copy_to(columns(s, u, q), tile_ref.at[q, samp, x],
                       send.at[q, ds, dx], recv.at[q, ds, dx], at(s, z, u))

    def issue(q, begin, end):
        @pl.when(q < CHUNKS)
        def _():
            @pl.loop(begin, end)
            def _(i):
                within(q, i).start()

    def landed(q):
        @pl.loop(1, others + 1)
        def _(turn):
            ds, dx = turn // X, lax.rem(turn, X)
            arrived(tile_ref.at[q, wrapped(samp - ds, GROUPS), wrapped(x - dx, X)],
                    send.at[q, ds, dx], recv.at[q, ds, dx])

    def own_copy(q):
        return pltpu.make_async_copy(columns(samp, x, q), tile_ref.at[q, samp, x], own_sem.at[q])

    def hop_copy(d, s, q):
        owner = wrapped(z - s, Z) if d == 0 else wrapped(z + s, Z)
        ref = pivot_ref.at[q, owner]
        return copy_to(ref, ref, zsend.at[d, s, q], zrecv.at[d, s, q],
                       at(samp, right if d == 0 else left, x))

    def came(d, s, q):
        owner = wrapped(z - 1 - s, Z) if d == 0 else wrapped(z + 1 + s, Z)
        arrived(pivot_ref.at[q, owner], zsend.at[d, s, q], zrecv.at[d, s, q])

    near[samp, x] = slot_ref[...]
    for ds, dx, peer in plane:
        start(copy_to(slot_ref, near.at[samp, x], ps.at[ds, dx], pr.at[ds, dx], peer))
    for q in range(CHUNKS):
        own_copy(q).start()
    for q in range(LEAD):
        issue(q, 0, others)

    for ds, dx, _ in plane:
        arrived(near.at[wrapped(samp - ds, GROUPS), wrapped(x - dx, X)],
                ps.at[ds, dx], pr.at[ds, dx])
    row = lax.broadcasted_iota(jnp.int32, (GROUPS, 128), 0)
    joined = jnp.zeros((GROUPS, 128), jnp.int32)
    for g in range(GROUPS):
        line = near[g, 0] + near[g, 1] + near[g, 2] + near[g, 3]
        joined = jnp.where(row == g, line, joined)
    slots_ref[z] = joined
    for dz, peer in column:
        ref = slots_ref.at[z]
        start(copy_to(ref, ref, zs.at[dz], zr.at[dz], peer))
    c_ref[...] = jnp.zeros_like(c_ref)
    p_ref[...] = jnp.zeros_like(p_ref)
    for dz, _ in column:
        arrived(slots_ref.at[wrapped(z - dz, Z)], zs.at[dz], zr.at[dz])
    wanted = lax.rem(lax.broadcasted_iota(jnp.int32, (n, 128), 0) + place_ref[1], n)
    for v in range(Z):
        line = jnp.sum(jnp.where(row == place_ref[0], slots_ref[v], 0), axis=0, keepdims=True)
        matched[:, v * 128 : v * 128 + 128] = jnp.where(wanted == line, 1.0, 0.0).astype(jnp.bfloat16)

    def products(q):
        part = n // 4
        raw = pivot_ref[q].reshape(n, wide)
        for i in range(4):
            ordered[i * part : i * part + part, :] = jnp.dot(
                matched[i * part : i * part + part, :], raw, preferred_element_type=jnp.float32
            ).astype(jnp.bfloat16)
        contract = (((1,), (1,)), ((), ()))
        whole = ordered[...]
        for i in range(Y):
            rows = tile_ref[q, 2 * i : 2 * i + 2].reshape(-1, wide)
            c_ref[i] = c_ref[i] + lax.dot_general(
                rows, whole, contract, preferred_element_type=jnp.float32
            ).reshape(c_ref.shape[1:])
        band = ordered[pl.ds(pl.multiple_of(z * 128, 128), 128), :]
        p_ref[...] = p_ref[...] + lax.dot_general(
            band, whole, contract, preferred_element_type=jnp.float32
        ).reshape(p_ref.shape)

    @pl.loop(0, CHUNKS + 4)
    def _(tick):
        @pl.when(tick < CHUNKS)
        def _():
            landed(tick)
            own_copy(tick).wait()
            picked = tile_ref[tick, 0]
            for g in range(1, GROUPS):
                picked = jnp.where(place_ref[0] == g, tile_ref[tick, g], picked)
            pivot_ref[tick, z] = picked
            for d in range(2):
                hop_copy(d, 0, tick).start()

        issue(tick + LEAD, 0, 8)
        for s in range(1, 4):
            q = tick - s

            @pl.when((q >= 0) & (q < CHUNKS))
            def _():
                for d in range(2):
                    came(d, s - 1, q)
                    if s < 3:
                        hop_copy(d, s, q).start()
                    else:
                        @pl.when(lax.rem(q, 2) == d)
                        def _():
                            hop_copy(d, s, q).start()

            issue(tick + LEAD, 8 * s, min(8 * s + 8, others))

        @pl.when(tick >= 4)
        def _():
            q = tick - 4
            for d in range(2):
                @pl.when(lax.rem(q, 2) == d)
                def _():
                    came(d, 3, q)
            products(q)

    @pl.loop(0, CHUNKS)
    def _(q):
        @pl.loop(0, others)
        def _(i):
            within(q, i).wait_send()
        for d in range(2):
            for s in range(3):
                hop_copy(d, s, q).wait_send()

            @pl.when(lax.rem(q, 2) == d)
            def _():
                hop_copy(d, 3, q).wait_send()

    for copy in sends:
        copy.wait_send()


def exchanged(jacobian, slots, place):
    vmem = pl.BlockSpec(memory_space=pltpu.VMEM)
    dma = pltpu.SemaphoreType.DMA
    rows, params = jacobian.shape
    wide = params // (GROUPS * X * CHUNKS)
    n = Z * X * rows
    f32, bf16 = jnp.float32, jnp.bfloat16
    return pl.pallas_call(
        exchange_kernel,
        out_shape=(
            jax.ShapeDtypeStruct((Y, 2, X, rows, n), f32),
            jax.ShapeDtypeStruct((Y, 2, 2, 8, n), f32),
            jax.ShapeDtypeStruct((Z, GROUPS, 128), slots.dtype),
        ),
        in_specs=[pl.BlockSpec(memory_space=pl.ANY), vmem,
                  pl.BlockSpec(memory_space=pltpu.SMEM)],
        out_specs=(vmem, vmem, vmem),
        scratch_shapes=[pltpu.VMEM((CHUNKS, GROUPS, X, rows, wide), bf16),
                        pltpu.VMEM((CHUNKS, Z, X, rows, wide), bf16),
                        pltpu.VMEM((GROUPS, X, 1, 128), slots.dtype),
                        pltpu.VMEM((n, n), bf16), pltpu.VMEM((n, wide), bf16),
                        dma((CHUNKS,)), dma((CHUNKS, GROUPS, X)), dma((CHUNKS, GROUPS, X)),
                        dma((2, 4, CHUNKS)), dma((2, 4, CHUNKS)),
                        dma((GROUPS, X)), dma((GROUPS, X)), dma((Z,)), dma((Z,))],
        compiler_params=pltpu.CompilerParams(collective_id=0, has_side_effects=True),
        name="exchange",
    )(jacobian, slots, place)


def reduce_kernel(p_ref, c_ref, pick_ref, place_ref, shift_ref, o_ref, g_ref,
                  got, piece, sib, acc, first0, first1, acc0, acc1, second0, second1,
                  part, column_rows, chosen, third,
                  ps, pr, zs, zr, xs, xr, ys, yr, ys2, yr2, xs2, xr2, cs, cr,
                  ss, sr, s0, r0, s1, r1, t0, q0, t1, q1, us, ur, vs, vr):
    samp, z, x = here()
    y, core = samp // 2, lax.rem(samp, 2)
    xh, xl = x // 2, lax.rem(x, 2)
    me, sibling = at(samp, z, x), at(2 * y + 1 - core, z, x)
    column, plane = column_peers(samp, z, x), plane_peers(samp, z, x)
    meet([peer for _, peer in column] + [peer for _, _, peer in plane])
    n = p_ref.shape[4]
    wide = n // 2
    low, high = pl.ds(0, wide), pl.ds(wide, wide)
    order = (2, 1, 3)
    sends = []

    def start(copy):
        copy.start()
        sends.append(copy)

    def arrived(ref, send, recv):
        copy_to(ref, ref, send, recv, me).wait_recv()

    def cols(xlow, color=None):
        if color is None:
            return pl.ds(pl.multiple_of(xlow * wide, wide), wide)
        return pl.ds(pl.multiple_of(xlow * wide + color * (wide // 2), wide // 2), wide // 2)

    def up(d):
        v = wrapped(y + d, Y)
        return v, at(2 * v + core, z, x)

    def along(d):
        u = wrapped(x + d, X)
        return u, at(samp, z, u)

    for ds, dx, peer in plane:
        s, u = wrapped(samp + ds, GROUPS), wrapped(x + dx, X)
        start(copy_to(p_ref.at[s // 2, lax.rem(s, 2), u // 2, :, cols(lax.rem(u, 2))],
                      got.at[ds, dx], ps.at[ds, dx], pr.at[ds, dx], peer))
    for d in order + (0,):
        v, _ = up(d)
        start(copy_to(c_ref.at[v, 1 - core], sib.at[v], ss.at[d], sr.at[d], sibling))
    for d in order + (0,):
        v, peer = up(d)
        arrived(sib.at[v], ss.at[d], sr.at[d])
        acc[v] = c_ref[v, core] + sib[v]
        if d:
            start(copy_to(acc.at[v, :, :, low], first0.at[d], s0.at[d], r0.at[d], peer))
    for d in order:
        u, peer = along(d)
        start(copy_to(acc.at[:, u, :, high], first1.at[d], s1.at[d], r1.at[d], peer))

    total = p_ref[y, core, xh, :, cols(xl)]
    for ds, dx, _ in plane:
        arrived(got.at[ds, dx], ps.at[ds, dx], pr.at[ds, dx])
    for ds, dx, _ in plane:
        total = total + got[ds, dx]
    shape = total.shape
    row = lax.broadcasted_iota(jnp.int32, shape, 0) + (z * 128 + (2 * samp + xh) * 8)
    column_id = lax.broadcasted_iota(jnp.int32, shape, 1) + xl * wide
    total = total / SAMPLES + jnp.where(row == column_id, shift_ref[0], 0.0)
    piece[...] = total
    o_ref[z, y, core, xh, :, cols(xl)] = total
    for dz, peer in column:
        start(copy_to(piece, o_ref.at[z, y, core, xh, :, cols(xl)], zs.at[dz], zr.at[dz], peer))
    for dz, _ in column:
        arrived(o_ref.at[wrapped(z - dz, Z), y, core, xh, :, cols(xl)], zs.at[dz], zr.at[dz])
    for d in order:
        ref0 = o_ref.at[:, y, core, xh, :, cols(xl, 0)]
        start(copy_to(ref0, ref0, xs.at[d], xr.at[d], along(d)[1]))
        ref1 = o_ref.at[:, y, core, xh, :, cols(xl, 1)]
        start(copy_to(ref1, ref1, ys.at[d], yr.at[d], up(d)[1]))

    for d in order:
        arrived(first0.at[d], s0.at[d], r0.at[d])
    acc0[...] = acc[y, :, :, low] + first0[1] + first0[2] + first0[3]
    for d in order:
        u, peer = along(d)
        start(copy_to(acc0.at[u], second0.at[d], t0.at[d], q0.at[d], peer))
    for d in order:
        arrived(first1.at[d], s1.at[d], r1.at[d])
    acc1[...] = acc[:, x, :, high] + first1[1] + first1[2] + first1[3]
    for d in order:
        v, peer = up(d)
        start(copy_to(acc1.at[v], second1.at[d], t1.at[d], q1.at[d], peer))

    for d in order:
        u = wrapped(x - d, X)
        arrived(o_ref.at[:, y, core, u // 2, :, cols(lax.rem(u, 2), 0)], xs.at[d], xr.at[d])
    for d in order:
        for half in range(2):
            ref = o_ref.at[:, y, core, :, :, cols(half, 0)]
            start(copy_to(ref, ref, ys2.at[d, half], yr2.at[d, half], up(d)[1]))
    for d in order:
        v = wrapped(y - d, Y)
        arrived(o_ref.at[:, v, core, xh, :, cols(xl, 1)], ys.at[d], yr.at[d])
    for d in order:
        ref = o_ref.at[:, :, core, xh, :, cols(xl, 1)]
        start(copy_to(ref, ref, xs2.at[d], xr2.at[d], along(d)[1]))

    for d in order:
        arrived(second0.at[d], t0.at[d], q0.at[d])
        arrived(second1.at[d], t1.at[d], q1.at[d])
    part[:, low] = acc0[x] + second0[1] + second0[2] + second0[3]
    part[:, high] = acc1[y] + second1[1] + second1[2] + second1[3]
    column_rows[z] = part[...]
    for dz, peer in column:
        start(copy_to(part, column_rows.at[z], us.at[dz], ur.at[dz], peer))

    for d in order:
        u = wrapped(x - d, X)
        arrived(o_ref.at[:, :, core, u // 2, :, cols(lax.rem(u, 2), 1)], xs2.at[d], xr2.at[d])
    for d in (0,) + order:
        v = wrapped(y - d, Y)
        if d:
            for half in range(2):
                arrived(o_ref.at[:, v, core, :, :, cols(half, 0)], ys2.at[d, half], yr2.at[d, half])
        ref = o_ref.at[:, v, core]
        start(copy_to(ref, ref, cs.at[d], cr.at[d], sibling))

    for dz, _ in column:
        arrived(column_rows.at[wrapped(z - dz, Z)], us.at[dz], ur.at[dz])
    rest = column_rows[...].reshape(pick_ref.shape[1], n)
    moved = jnp.zeros((pick_ref.shape[0], n), jnp.float32)
    for _ in range(3):
        head = rest.astype(jnp.bfloat16)
        rest = rest - head.astype(jnp.float32)
        moved = moved + lax.dot_general(
            pick_ref[...], head, (((1,), (0,)), ((), ())), preferred_element_type=jnp.float32
        )
    chosen[...] = moved.reshape(chosen.shape)
    for d in order:
        u, peer = along(d)
        start(copy_to(chosen.at[u], third.at[d], vs.at[d], vr.at[d], peer))
    width = chosen.shape[1]
    position = lax.broadcasted_iota(jnp.int32, (width, n), 0) + (z * X + x) * width
    column_id = lax.broadcasted_iota(jnp.int32, (width, n), 1)
    on_pivot = jnp.where(position == lax.rem(column_id + place_ref[1], n), shift_ref[0], 0.0)
    on_pivot = jnp.where(place_ref[0] == samp, on_pivot, 0.0)
    for d in order:
        arrived(third.at[d], vs.at[d], vr.at[d])
    g_ref[...] = (chosen[x] + third[1] + third[2] + third[3]) / SAMPLES + on_pivot
    for d in range(Y):
        arrived(o_ref.at[:, wrapped(y - d, Y), 1 - core], cs.at[d], cr.at[d])
    for copy in sends:
        copy.wait_send()


def reduced(part, partial, pick, place, shift):
    vmem = pl.BlockSpec(memory_space=pltpu.VMEM)
    smem = pl.BlockSpec(memory_space=pltpu.SMEM)
    dma = pltpu.SemaphoreType.DMA
    rows, n = partial.shape[3:]
    wide = n // 2
    f32 = jnp.float32
    block, my_rows = pl.pallas_call(
        reduce_kernel,
        out_shape=(jax.ShapeDtypeStruct((Z, Y, 2, 2, 8, n), f32),
                   jax.ShapeDtypeStruct((rows, n), f32)),
        in_specs=[vmem, vmem, vmem, smem, smem],
        out_specs=(vmem, vmem),
        scratch_shapes=[
            pltpu.VMEM((GROUPS, X, 8, wide), f32), pltpu.VMEM((8, wide), f32),
            pltpu.VMEM((Y, X, rows, n), f32), pltpu.VMEM((Y, X, rows, n), f32),
            pltpu.VMEM((Y, X, rows, wide), f32), pltpu.VMEM((X, Y, rows, wide), f32),
            pltpu.VMEM((X, rows, wide), f32), pltpu.VMEM((Y, rows, wide), f32),
            pltpu.VMEM((X, rows, wide), f32), pltpu.VMEM((Y, rows, wide), f32),
            pltpu.VMEM((rows, n), f32), pltpu.VMEM((Z, rows, n), f32),
            pltpu.VMEM((X, rows, n), f32), pltpu.VMEM((X, rows, n), f32),
            dma((GROUPS, X)), dma((GROUPS, X)), dma((Z,)), dma((Z,)),
            dma((4,)), dma((4,)), dma((4,)), dma((4,)),
            dma((4, 2)), dma((4, 2)), dma((4,)), dma((4,)), dma((4,)), dma((4,)),
        ] + [dma((4,))] * 10 + [dma((Z,)), dma((Z,)), dma((4,)), dma((4,))],
        compiler_params=pltpu.CompilerParams(collective_id=1, has_side_effects=True),
        name="reduce",
    )(part, partial, pick, place, shift)
    return block.reshape(n, n), my_rows


def on_device(jacobian, sample_slot, panel_index, shift_value):
    width = sample_slot.shape[0]
    group_width = width * lax.axis_size(PAR)
    pivot_group = panel_index[0] // group_width
    rotation = panel_index[0] % group_width
    band = group_width // lax.axis_size("z")
    lanes = jnp.tile(sample_slot, X).reshape(1, width * X)
    own_lanes = jnp.arange(width * X, dtype=jnp.int32)[None, :] // width == lax.axis_index("x")
    padded = jnp.where(own_lanes, lanes, 0)
    place = jnp.stack([pivot_group, rotation])
    partial, pivot_part, slots = exchanged(jacobian, padded, place)
    own_slots = lax.dynamic_index_in_dim(slots, lax.axis_index("samp"), 1, keepdims=False)
    sources = own_slots.reshape(-1, X, width)
    sources = lax.dynamic_index_in_dim(sources, lax.axis_index("x"), 1, keepdims=False)
    target = lax.axis_index("z") * band + jnp.arange(band, dtype=jnp.int32)
    pick = (target[:, None] == sources.reshape(1, -1)).astype(jnp.bfloat16)
    block, my_rows = reduced(pivot_part, partial, pick, place, shift_value)
    return solved(my_rows, block)


def solution(mesh):
    torus = Mesh(mesh.devices.reshape(mesh.shape["samp"], 8, 4), ("samp", "z", "x"))
    return jax.shard_map(
        on_device,
        mesh=torus,
        in_specs=(P(ALL, None), P(ALL), P(), P()),
        out_specs=P(ALL, None),
        check_vma=False,
    )
```

```python
import functools

import jax
import jax.numpy as jnp
from jax import lax
from jax.experimental import pallas as pl
from jax.experimental.pallas import tpu as pltpu
from jax.sharding import Mesh
from jax.sharding import PartitionSpec as P

PAR = ("z", "x")
PLANE = ("samp", "x")
ALL = ("samp", "z", "x")
NB = 128
STEP = 16
HI = lax.Precision.HIGHEST


def rank_update(r):
    h = r.astype(jnp.bfloat16).astype(jnp.float32)
    m = (r - h).astype(jnp.bfloat16).astype(jnp.float32)
    l = (r - h - m).astype(jnp.bfloat16).astype(jnp.float32)
    lhs = jnp.concatenate([h, h, m, h, l, m], 0).astype(jnp.bfloat16)
    rhs = jnp.concatenate([h, m, h, l, h, m], 0).astype(jnp.bfloat16)
    return lax.dot_general(
        lhs, rhs, (((0,), (0,)), ((), ())), preferred_element_type=jnp.float32
    )


def inverse_of_factor(block, filler):
    n = block.shape[0]
    groups = n // STEP
    rows = [block[STEP * i : STEP * i + STEP, :] for i in range(groups)]
    sub = lax.broadcasted_iota(jnp.int32, (STEP, n), 0)
    lane = lax.broadcasted_iota(jnp.int32, (STEP, n), 1)
    for b in range(groups):
        first = STEP * b
        r = rows[b]
        cols = [jnp.broadcast_to(r[:, first + j : first + j + 1], (STEP, n)) for j in range(STEP)]
        inside = (lane >= first) & (lane < first + STEP)
        r = jnp.where(inside, jnp.where(lane == sub + first, 1.0, 0.0), r)
        diag = jnp.ones((STEP, n), jnp.float32)
        for j in range(STEP):
            d = jnp.broadcast_to(cols[j][j : j + 1, :], (8, n))
            diag = jnp.where(sub == j, jnp.concatenate([d] * (STEP // 8), 0), diag)
            if j == STEP - 1:
                break
            low = (j + 1) // 8 * 8
            below = (STEP - low) // 8
            q = pl.reciprocal(d, approx=True)
            e = jnp.concatenate([1.0 - d * q] * below, 0)
            m = jnp.where(sub[low:] > j, cols[j][low:], 0.0) * jnp.concatenate([q] * below, 0)
            m = m + m * e

            def eliminated(v):
                left = v[low:] - m * jnp.broadcast_to(v[j : j + 1, :], (STEP - low, n))
                return left if low == 0 else jnp.concatenate([v[:low], left], 0)

            for c in range(j + 1, STEP):
                cols[c] = eliminated(cols[c])
            r = eliminated(r)
        s = lax.rsqrt(diag)
        s = s * (1.5 - 0.5 * diag * s * s)
        r = r * s
        rows[b] = r
        if b < groups - 1:
            p = rank_update(r)
            for i in range(b + 1, groups):
                rows[i] = jnp.where(inside, 0.0, rows[i]) - p[STEP * i : STEP * i + STEP, :]
        filler()
    kept = [jnp.where(lane <= sub + STEP * b, rows[b], 0.0) for b in range(groups)]
    return jnp.concatenate(kept, 0)


def times_transposed(a, b):
    return lax.dot_general(
        a, b, (((1,), (1,)), ((), ())), precision=HI, preferred_element_type=jnp.float32
    )


def factor_kernel(a_ref, g_ref, x_ref, o_ref):
    n = a_ref.shape[0]
    steps = n // NB
    waiting = []

    def run(count):
        for _ in range(min(count, len(waiting))):
            waiting.pop(0)()

    x_ref[...] = g_ref[...]
    for kb in range(steps):
        s_ref = a_ref if kb == 0 else o_ref
        own = slice(kb * NB, kb * NB + NB)
        share = -(-len(waiting) // (NB // STEP))
        w = inverse_of_factor(s_ref[own, own], lambda: run(share))
        run(len(waiting))
        lo = (kb + 1) * NB
        x_ref[:, own] = times_transposed(x_ref[:, own], w)
        if kb == steps - 1:
            break
        o_ref[lo:, own] = times_transposed(s_ref[lo:, own], w)

        def update(j, top, end, s_ref=s_ref, own=own):
            cj = slice(j * NB, j * NB + NB)
            o_ref[top:end, cj] = s_ref[top:end, cj] - times_transposed(
                o_ref[top:end, own], o_ref[cj, own]
            )

        def advance(left, end, own=own):
            x_ref[:, left:end] = x_ref[:, left:end] - times_transposed(
                x_ref[:, own], o_ref[left:end, own]
            )

        update(kb + 1, lo, n)
        waiting.append(functools.partial(advance, lo, n))
        for j in range(kb + 2, steps):
            for top in range(j * NB, n, 2 * NB):
                waiting.append(functools.partial(update, j, top, min(n, top + 2 * NB)))


def solved(rows, block):
    vmem = pl.BlockSpec(memory_space=pltpu.VMEM)
    return pl.pallas_call(
        factor_kernel,
        out_shape=jax.ShapeDtypeStruct(rows.shape, jnp.float32),
        in_specs=[vmem, vmem],
        out_specs=vmem,
        scratch_shapes=[pltpu.VMEM(block.shape, jnp.float32)],
        name="factor",
    )(block, rows)


MESH_IDS = pl.DeviceIdType.MESH
Z, X, Y, GROUPS = 8, 4, 4, 8
CHUNKS = 8
SAMPLES = 8192
LEAD = 2


def here():
    samp, z, x = lax.axis_index("samp"), lax.axis_index("z"), lax.axis_index("x")
    return samp, z, x


def wrapped(value, size):
    return lax.rem(value + size, size)


def meet(peers):
    barrier = pltpu.get_barrier_semaphore()
    for peer in peers:
        pl.semaphore_signal(barrier, inc=1, device_id=peer, device_id_type=MESH_IDS)
    pl.semaphore_wait(barrier, len(peers))


def at(samp, z, x):
    return {"samp": samp, "z": z, "x": x}


def plane_peers(samp, z, x):
    return [
        (ds, dx, at(wrapped(samp + ds, GROUPS), z, wrapped(x + dx, X)))
        for ds in range(GROUPS)
        for dx in range(X)
        if (ds, dx) != (0, 0)
    ]


def column_peers(samp, z, x):
    return [(dz, at(samp, wrapped(z + dz, Z), x)) for dz in range(1, Z)]


def copy_to(src, dst, send, recv, peer):
    return pltpu.make_async_remote_copy(
        src_ref=src, dst_ref=dst, send_sem=send, recv_sem=recv,
        device_id=peer, device_id_type=MESH_IDS,
    )


def exchange_kernel(jac_ref, slot_ref, place_ref, c_ref, p_ref, slots_ref,
                    tile_ref, pivot_ref, near, matched, ordered,
                    own_sem, send, recv, zsend, zrecv, ps, pr, zs, zr):
    samp, z, x = here()
    right, left = wrapped(z + 1, Z), wrapped(z - 1, Z)
    column, plane = column_peers(samp, z, x), plane_peers(samp, z, x)
    me = at(samp, z, x)
    meet([peer for _, peer in column] + [peer for _, _, peer in plane])
    wide = tile_ref.shape[-1]
    n = ordered.shape[0]
    others = GROUPS * X - 1
    sends = []

    def start(copy):
        copy.start()
        sends.append(copy)

    def arrived(ref, send_sem, recv_sem):
        copy_to(ref, ref, send_sem, recv_sem, me).wait_recv()

    def columns(s, u, q):
        first = pl.multiple_of(((s * X + u) * CHUNKS + q) * wide, wide)
        return jac_ref.at[:, pl.ds(first, wide)]

    def within(q, i):
        turn = lax.rem(7 * i, others) + 1
        ds, dx = turn // X, lax.rem(turn, X)
        s, u = wrapped(samp + ds, GROUPS), wrapped(x + dx, X)
        return copy_to(columns(s, u, q), tile_ref.at[q, samp, x],
                       send.at[q, ds, dx], recv.at[q, ds, dx], at(s, z, u))

    def issue(q, begin, end):
        @pl.when(q < CHUNKS)
        def _():
            @pl.loop(begin, end)
            def _(i):
                within(q, i).start()

    def landed(q):
        @pl.loop(1, others + 1)
        def _(turn):
            ds, dx = turn // X, lax.rem(turn, X)
            arrived(tile_ref.at[q, wrapped(samp - ds, GROUPS), wrapped(x - dx, X)],
                    send.at[q, ds, dx], recv.at[q, ds, dx])

    def own_copy(q):
        return pltpu.make_async_copy(columns(samp, x, q), tile_ref.at[q, samp, x], own_sem.at[q])

    def hop_copy(d, s, q):
        owner = wrapped(z - s, Z) if d == 0 else wrapped(z + s, Z)
        ref = pivot_ref.at[q, owner]
        return copy_to(ref, ref, zsend.at[d, s, q], zrecv.at[d, s, q],
                       at(samp, right if d == 0 else left, x))

    def came(d, s, q):
        owner = wrapped(z - 1 - s, Z) if d == 0 else wrapped(z + 1 + s, Z)
        arrived(pivot_ref.at[q, owner], zsend.at[d, s, q], zrecv.at[d, s, q])

    near[samp, x] = slot_ref[...]
    for ds, dx, peer in plane:
        start(copy_to(slot_ref, near.at[samp, x], ps.at[ds, dx], pr.at[ds, dx], peer))
    for q in range(CHUNKS):
        own_copy(q).start()
    for q in range(LEAD):
        issue(q, 0, others)

    for ds, dx, _ in plane:
        arrived(near.at[wrapped(samp - ds, GROUPS), wrapped(x - dx, X)],
                ps.at[ds, dx], pr.at[ds, dx])
    row = lax.broadcasted_iota(jnp.int32, (GROUPS, 128), 0)
    joined = jnp.zeros((GROUPS, 128), jnp.int32)
    for g in range(GROUPS):
        line = near[g, 0] + near[g, 1] + near[g, 2] + near[g, 3]
        joined = jnp.where(row == g, line, joined)
    slots_ref[z] = joined
    for dz, peer in column:
        ref = slots_ref.at[z]
        start(copy_to(ref, ref, zs.at[dz], zr.at[dz], peer))
    c_ref[...] = jnp.zeros_like(c_ref)
    p_ref[...] = jnp.zeros_like(p_ref)
    for dz, _ in column:
        arrived(slots_ref.at[wrapped(z - dz, Z)], zs.at[dz], zr.at[dz])
    wanted = lax.rem(lax.broadcasted_iota(jnp.int32, (n, 128), 0) + place_ref[1], n)
    for v in range(Z):
        line = jnp.sum(jnp.where(row == place_ref[0], slots_ref[v], 0), axis=0, keepdims=True)
        matched[:, v * 128 : v * 128 + 128] = jnp.where(wanted == line, 1.0, 0.0).astype(jnp.bfloat16)

    def products(q):
        part = n // 4
        raw = pivot_ref[q].reshape(n, wide)
        for i in range(4):
            ordered[i * part : i * part + part, :] = jnp.dot(
                matched[i * part : i * part + part, :], raw, preferred_element_type=jnp.float32
            ).astype(jnp.bfloat16)
        contract = (((1,), (1,)), ((), ()))
        whole = ordered[...]
        for i in range(Y):
            rows = tile_ref[q, 2 * i : 2 * i + 2].reshape(-1, wide)
            c_ref[i] = c_ref[i] + lax.dot_general(
                rows, whole, contract, preferred_element_type=jnp.float32
            ).reshape(c_ref.shape[1:])
        band = ordered[pl.ds(pl.multiple_of(z * 128, 128), 128), :]
        p_ref[...] = p_ref[...] + lax.dot_general(
            band, whole, contract, preferred_element_type=jnp.float32
        ).reshape(p_ref.shape)

    @pl.loop(0, CHUNKS + 4)
    def _(tick):
        @pl.when(tick < CHUNKS)
        def _():
            landed(tick)
            own_copy(tick).wait()
            picked = tile_ref[tick, 0]
            for g in range(1, GROUPS):
                picked = jnp.where(place_ref[0] == g, tile_ref[tick, g], picked)
            pivot_ref[tick, z] = picked
            for d in range(2):
                hop_copy(d, 0, tick).start()

        issue(tick + LEAD, 0, 8)
        for s in range(1, 4):
            q = tick - s

            @pl.when((q >= 0) & (q < CHUNKS))
            def _():
                for d in range(2):
                    came(d, s - 1, q)
                    if s < 3:
                        hop_copy(d, s, q).start()
                    else:
                        @pl.when(lax.rem(q, 2) == d)
                        def _():
                            hop_copy(d, s, q).start()

            issue(tick + LEAD, 8 * s, min(8 * s + 8, others))

        @pl.when(tick >= 4)
        def _():
            q = tick - 4
            for d in range(2):
                @pl.when(lax.rem(q, 2) == d)
                def _():
                    came(d, 3, q)
            products(q)

    @pl.loop(0, CHUNKS)
    def _(q):
        @pl.loop(0, others)
        def _(i):
            within(q, i).wait_send()
        for d in range(2):
            for s in range(3):
                hop_copy(d, s, q).wait_send()

            @pl.when(lax.rem(q, 2) == d)
            def _():
                hop_copy(d, 3, q).wait_send()

    for copy in sends:
        copy.wait_send()


def exchanged(jacobian, slots, place):
    vmem = pl.BlockSpec(memory_space=pltpu.VMEM)
    dma = pltpu.SemaphoreType.DMA
    rows, params = jacobian.shape
    wide = params // (GROUPS * X * CHUNKS)
    n = Z * X * rows
    f32, bf16 = jnp.float32, jnp.bfloat16
    return pl.pallas_call(
        exchange_kernel,
        out_shape=(
            jax.ShapeDtypeStruct((Y, 2, X, rows, n), f32),
            jax.ShapeDtypeStruct((Y, 2, 2, 8, n), f32),
            jax.ShapeDtypeStruct((Z, GROUPS, 128), slots.dtype),
        ),
        in_specs=[pl.BlockSpec(memory_space=pl.ANY), vmem,
                  pl.BlockSpec(memory_space=pltpu.SMEM)],
        out_specs=(vmem, vmem, vmem),
        scratch_shapes=[pltpu.VMEM((CHUNKS, GROUPS, X, rows, wide), bf16),
                        pltpu.VMEM((CHUNKS, Z, X, rows, wide), bf16),
                        pltpu.VMEM((GROUPS, X, 1, 128), slots.dtype),
                        pltpu.VMEM((n, n), bf16), pltpu.VMEM((n, wide), bf16),
                        dma((CHUNKS,)), dma((CHUNKS, GROUPS, X)), dma((CHUNKS, GROUPS, X)),
                        dma((2, 4, CHUNKS)), dma((2, 4, CHUNKS)),
                        dma((GROUPS, X)), dma((GROUPS, X)), dma((Z,)), dma((Z,))],
        compiler_params=pltpu.CompilerParams(collective_id=0, has_side_effects=True),
        name="exchange",
    )(jacobian, slots, place)


def reduce_kernel(p_ref, c_ref, pick_ref, place_ref, shift_ref, o_ref, g_ref,
                  got, piece, sib, acc, first0, first1, acc0, acc1, second0, second1,
                  column_rows, chosen, third,
                  ps, pr, zs, zr, xs, xr, ys, yr, ys2, yr2, xs2, xr2, cs, cr,
                  ss, sr, s0, r0, s1, r1, t0, q0, t1, q1, us, ur, vs, vr):
    samp, z, x = here()
    y, core = samp // 2, lax.rem(samp, 2)
    xh, xl = x // 2, lax.rem(x, 2)
    me, sibling = at(samp, z, x), at(2 * y + 1 - core, z, x)
    column, plane = column_peers(samp, z, x), plane_peers(samp, z, x)
    meet([peer for _, peer in column] + [peer for _, _, peer in plane])
    n = p_ref.shape[4]
    wide = n // 2
    narrow = wide // X
    low = pl.ds(0, wide)

    def share(u, half):
        return pl.ds(pl.multiple_of(half * wide + u * narrow, narrow), narrow)

    order = (2, 1, 3)
    sends = []

    def start(copy):
        copy.start()
        sends.append(copy)

    def arrived(ref, send, recv):
        copy_to(ref, ref, send, recv, me).wait_recv()

    def cols(xlow, color=None):
        if color is None:
            return pl.ds(pl.multiple_of(xlow * wide, wide), wide)
        return pl.ds(pl.multiple_of(xlow * wide + color * (wide // 2), wide // 2), wide // 2)

    def up(d):
        v = wrapped(y + d, Y)
        return v, at(2 * v + core, z, x)

    def along(d):
        u = wrapped(x + d, X)
        return u, at(samp, z, u)

    for ds, dx, peer in plane:
        s, u = wrapped(samp + ds, GROUPS), wrapped(x + dx, X)
        start(copy_to(p_ref.at[s // 2, lax.rem(s, 2), u // 2, :, cols(lax.rem(u, 2))],
                      got.at[ds, dx], ps.at[ds, dx], pr.at[ds, dx], peer))
    for d in order + (0,):
        v, _ = up(d)
        start(copy_to(c_ref.at[v, 1 - core], sib.at[v], ss.at[d], sr.at[d], sibling))
    for d in order + (0,):
        v, peer = up(d)
        arrived(sib.at[v], ss.at[d], sr.at[d])
        acc[v] = c_ref[v, core] + sib[v]
        if d:
            start(copy_to(acc.at[v, :, :, low], first0.at[d], s0.at[d], r0.at[d], peer))
    for d in order:
        u, peer = along(d)
        start(copy_to(acc.at[:, :, :, share(u, 1)], first1.at[d], s1.at[d], r1.at[d], peer))

    total = p_ref[y, core, xh, :, cols(xl)]
    for ds, dx, _ in plane:
        arrived(got.at[ds, dx], ps.at[ds, dx], pr.at[ds, dx])
    for ds, dx, _ in plane:
        total = total + got[ds, dx]
    shape = total.shape
    row = lax.broadcasted_iota(jnp.int32, shape, 0) + (z * 128 + (2 * samp + xh) * 8)
    column_id = lax.broadcasted_iota(jnp.int32, shape, 1) + xl * wide
    total = total / SAMPLES + jnp.where(row == column_id, shift_ref[0], 0.0)
    piece[...] = total
    o_ref[z, y, core, xh, :, cols(xl)] = total
    for dz, peer in column:
        start(copy_to(piece, o_ref.at[z, y, core, xh, :, cols(xl)], zs.at[dz], zr.at[dz], peer))
    for dz, _ in column:
        arrived(o_ref.at[wrapped(z - dz, Z), y, core, xh, :, cols(xl)], zs.at[dz], zr.at[dz])
    for d in order:
        ref0 = o_ref.at[:, y, core, xh, :, cols(xl, 0)]
        start(copy_to(ref0, ref0, xs.at[d], xr.at[d], along(d)[1]))
        ref1 = o_ref.at[:, y, core, xh, :, cols(xl, 1)]
        start(copy_to(ref1, ref1, ys.at[d], yr.at[d], up(d)[1]))

    for d in order:
        arrived(first0.at[d], s0.at[d], r0.at[d])
    acc0[...] = acc[y, :, :, low] + first0[1] + first0[2] + first0[3]
    for d in order:
        u, peer = along(d)
        start(copy_to(acc0.at[:, :, share(u, 0)], second0.at[d], t0.at[d], q0.at[d], peer))
    for d in order:
        arrived(first1.at[d], s1.at[d], r1.at[d])
    acc1[...] = acc[:, :, :, share(x, 1)] + first1[1] + first1[2] + first1[3]
    for d in order:
        v, peer = up(d)
        start(copy_to(acc1.at[v], second1.at[d], t1.at[d], q1.at[d], peer))

    for d in order:
        u = wrapped(x - d, X)
        arrived(o_ref.at[:, y, core, u // 2, :, cols(lax.rem(u, 2), 0)], xs.at[d], xr.at[d])
    for d in order:
        for half in range(2):
            ref = o_ref.at[:, y, core, :, :, cols(half, 0)]
            start(copy_to(ref, ref, ys2.at[d, half], yr2.at[d, half], up(d)[1]))
    for d in order:
        v = wrapped(y - d, Y)
        arrived(o_ref.at[:, v, core, xh, :, cols(xl, 1)], ys.at[d], yr.at[d])
    for d in order:
        ref = o_ref.at[:, :, core, xh, :, cols(xl, 1)]
        start(copy_to(ref, ref, xs2.at[d], xr2.at[d], along(d)[1]))

    for d in order:
        arrived(second0.at[d], t0.at[d], q0.at[d])
        arrived(second1.at[d], t1.at[d], q1.at[d])
    column_rows[z, :, :, pl.ds(0, narrow)] = (
        acc0[:, :, share(x, 0)] + second0[1] + second0[2] + second0[3])
    column_rows[z, :, :, pl.ds(narrow, narrow)] = acc1[y] + second1[1] + second1[2] + second1[3]

    def half_of(owner, h):
        return column_rows.at[owner, pl.ds(h * (X // 2), X // 2)]

    def hop(s):
        for h in range(2):
            for d in range(2):
                if s > 0:
                    came(d, s - 1, h)
                if s < 3 or h == d:
                    owner = wrapped(z - s, Z) if d == 0 else wrapped(z + s, Z)
                    to = at(samp, wrapped(z + 1, Z) if d == 0 else wrapped(z - 1, Z), x)
                    ref = half_of(owner, h)
                    start(copy_to(ref, ref, us.at[d, s, h], ur.at[d, s, h], to))

    def came(d, s, h):
        owner = wrapped(z - 1 - s, Z) if d == 0 else wrapped(z + 1 + s, Z)
        arrived(half_of(owner, h), us.at[d, s, h], ur.at[d, s, h])

    hop(0)
    hop(1)
    hop(2)

    for d in order:
        u = wrapped(x - d, X)
        arrived(o_ref.at[:, :, core, u // 2, :, cols(lax.rem(u, 2), 1)], xs2.at[d], xr2.at[d])
    for d in (0,) + order:
        v = wrapped(y - d, Y)
        if d:
            for half in range(2):
                arrived(o_ref.at[:, v, core, :, :, cols(half, 0)], ys2.at[d, half], yr2.at[d, half])
        ref = o_ref.at[:, v, core]
        start(copy_to(ref, ref, cs.at[d], cr.at[d], sibling))

    hop(3)
    for d in range(2):
        came(d, 3, d)
    rest = column_rows[...].reshape(pick_ref.shape[1], 2 * narrow)
    moved = jnp.zeros((pick_ref.shape[0], 2 * narrow), jnp.float32)
    for _ in range(3):
        head = rest.astype(jnp.bfloat16)
        rest = rest - head.astype(jnp.float32)
        moved = moved + lax.dot_general(
            pick_ref[...], head, (((1,), (0,)), ((), ())), preferred_element_type=jnp.float32
        )
    chosen[...] = moved.reshape(chosen.shape)
    for d in order:
        u, peer = along(d)
        start(copy_to(chosen.at[u], third.at[d], vs.at[d], vr.at[d], peer))
    width = chosen.shape[1]
    position = lax.broadcasted_iota(jnp.int32, (width, narrow), 0) + (z * X + x) * width

    def finish(u, values):
        for half in range(2):
            to = share(u, half)
            piece_columns = lax.broadcasted_iota(jnp.int32, (width, narrow), 1)
            piece_columns = piece_columns + (half * wide + u * narrow)
            added = jnp.where(position == lax.rem(piece_columns + place_ref[1], n), shift_ref[0], 0.0)
            added = jnp.where(place_ref[0] == samp, added, 0.0)
            g_ref[:, to] = values[:, half * narrow : half * narrow + narrow] / SAMPLES + added

    finish(x, chosen[x])
    for d in order:
        arrived(third.at[d], vs.at[d], vr.at[d])
        finish(wrapped(x - d, X), third[d])
    for d in range(Y):
        arrived(o_ref.at[:, wrapped(y - d, Y), 1 - core], cs.at[d], cr.at[d])
    for copy in sends:
        copy.wait_send()


def reduced(part, partial, pick, place, shift):
    vmem = pl.BlockSpec(memory_space=pltpu.VMEM)
    smem = pl.BlockSpec(memory_space=pltpu.SMEM)
    dma = pltpu.SemaphoreType.DMA
    rows, n = partial.shape[3:]
    wide = n // 2
    f32 = jnp.float32
    block, my_rows = pl.pallas_call(
        reduce_kernel,
        out_shape=(jax.ShapeDtypeStruct((Z, Y, 2, 2, 8, n), f32),
                   jax.ShapeDtypeStruct((rows, n), f32)),
        in_specs=[vmem, vmem, vmem, smem, smem],
        out_specs=(vmem, vmem),
        scratch_shapes=[
            pltpu.VMEM((GROUPS, X, 8, wide), f32), pltpu.VMEM((8, wide), f32),
            pltpu.VMEM((Y, X, rows, n), f32), pltpu.VMEM((Y, X, rows, n), f32),
            pltpu.VMEM((Y, X, rows, wide), f32), pltpu.VMEM((X, Y, X, rows, wide // X), f32),
            pltpu.VMEM((X, rows, wide), f32), pltpu.VMEM((Y, X, rows, wide // X), f32),
            pltpu.VMEM((X, X, rows, wide // X), f32), pltpu.VMEM((Y, X, rows, wide // X), f32),
            pltpu.VMEM((Z, X, rows, n // X), f32),
            pltpu.VMEM((X, rows, n // X), f32), pltpu.VMEM((X, rows, n // X), f32),
            dma((GROUPS, X)), dma((GROUPS, X)), dma((Z,)), dma((Z,)),
            dma((4,)), dma((4,)), dma((4,)), dma((4,)),
            dma((4, 2)), dma((4, 2)), dma((4,)), dma((4,)), dma((4,)), dma((4,)),
        ] + [dma((4,))] * 10 + [dma((2, 4, 2)), dma((2, 4, 2)), dma((4,)), dma((4,))],
        compiler_params=pltpu.CompilerParams(collective_id=1, has_side_effects=True),
        name="reduce",
    )(part, partial, pick, place, shift)
    return block.reshape(n, n), my_rows


def on_device(jacobian, sample_slot, panel_index, shift_value):
    width = sample_slot.shape[0]
    group_width = width * lax.axis_size(PAR)
    pivot_group = panel_index[0] // group_width
    rotation = panel_index[0] % group_width
    band = group_width // lax.axis_size("z")
    lanes = jnp.tile(sample_slot, X).reshape(1, width * X)
    own_lanes = jnp.arange(width * X, dtype=jnp.int32)[None, :] // width == lax.axis_index("x")
    padded = jnp.where(own_lanes, lanes, 0)
    place = jnp.stack([pivot_group, rotation])
    partial, pivot_part, slots = exchanged(jacobian, padded, place)
    own_slots = lax.dynamic_index_in_dim(slots, lax.axis_index("samp"), 1, keepdims=False)
    target = lax.axis_index("z") * band + jnp.arange(band, dtype=jnp.int32)
    pick = (target[:, None] == own_slots.reshape(1, -1)).astype(jnp.bfloat16)
    block, my_rows = reduced(pivot_part, partial, pick, place, shift_value)
    return solved(my_rows, block)


def solution(mesh):
    torus = Mesh(mesh.devices.reshape(mesh.shape["samp"], 8, 4), ("samp", "z", "x"))
    return jax.shard_map(
        on_device,
        mesh=torus,
        in_specs=(P(ALL, None), P(ALL), P(), P()),
        out_specs=P(ALL, None),
        check_vma=False,
    )
```
